256 devices in a mesh: seg: 32 (over x, z), tok: 8 (over y, core).
Axes of the slice: x: 4, y: 4, z: 8, core: 2. Of those that a mesh axis runs over, the one named last changes fastest.
Arguments:
- queries: bfloat16 [65536, 2048], P(('seg', 'tok')), may hold values from -40 to 40
- keys: bfloat16 [65536, 512], P(('seg', 'tok')), may hold values from -40 to 40
- values: bfloat16 [65536, 512], P(('seg', 'tok')), may hold values from -6 to 6
- gain_mem: float32 [2048], replicated, may hold values from 0.25 to 1.75
- gain_dot: float32 [2048], replicated, may hold values from 0.25 to 1.75
- out_weight: bfloat16 [2048, 2048], replicated, may hold values from -0.125 to 0.125
Outputs:
- layer_out: bfloat16 [65536, 2048], P(('seg', 'tok'))
The draws below stay inside these ranges and needn't reach their ends.
All inputs are finite; a program needn't handle non-finite values.
Results may differ from the reference program's by a relative error of at most 0.008.
Values may be sent and summed in bfloat16 or wider, within the bound.
No kernel may reach another device: no remote copies, remote signals or barrier semaphores. Data moves between devices by JAX's collectives and lax.ppermute only.
A program may use at most 128 MiB of HBM per device.

```python
import jax
import jax.numpy as jnp
from jax import lax

QUERY_HEADS = 16
KEY_VALUE_HEADS = 4
HEAD_DIMENSION = 128
D = 2048
SEGMENT_TOKENS = 2048
TOTAL_TOKENS = 65536


def draw_keys(key, part):
    random_sample = jax.random.truncated_normal(jax.random.fold_in(key, 3), -6.0, 6.0, (TOTAL_TOKENS, KEY_VALUE_HEADS * HEAD_DIMENSION), jnp.float32)
    return random_sample.astype(jnp.bfloat16)


def draw_queries(key, part):
    random_sample = jax.random.truncated_normal(jax.random.fold_in(key, 4), -6.0, 6.0, (TOTAL_TOKENS, QUERY_HEADS * HEAD_DIMENSION), jnp.float32)
    return random_sample.astype(jnp.bfloat16)


def shard_levels(key, dims, split, low, high):
    def one(position, shards_of):
        steps = jax.random.uniform(jax.random.fold_in(jax.random.fold_in(key, 6), position), (shards_of,), jnp.float32, low / len(split), high / len(split))
        return jnp.repeat(jnp.exp(steps), dims[position] // shards_of).reshape((-1,) + (1,) * (len(dims) - position - 1))

    level = one(*split[0])
    for cut in split[1:]:
        level = level * one(*cut)
    return level


def centred(key, dims, width, limit, pieces=(), kind=jnp.bfloat16):
    array = width * jax.random.normal(key, dims, jnp.float32)
    if pieces:
        array = array * shard_levels(key, dims, pieces, -0.22, 0.18)
    return jnp.clip(array, -limit, limit).astype(kind)


def setup_inputs(seed: int = 0) -> dict:
    arg_keys = jax.random.split(jax.random.key(seed), 7)
    queries = draw_queries(jax.random.fold_in(arg_keys[6], 71), 0)
    keys = draw_keys(jax.random.fold_in(arg_keys[6], 71), 0)
    values = centred(arg_keys[2], (TOTAL_TOKENS, KEY_VALUE_HEADS * HEAD_DIMENSION), 1.0, 6.0, ((0, 256),))
    gain_mem = jnp.clip(1.0 + 0.15 * jax.random.normal(arg_keys[3], (D,), jnp.float32), 0.25, 1.75)
    gain_dot = jnp.clip(1.0 + 0.15 * jax.random.normal(arg_keys[4], (D,), jnp.float32), 0.25, 1.75)
    out_weight = centred(arg_keys[5], (D, D), D ** -0.5, 0.125)
    return {"queries": queries, "keys": keys, "values": values, "gain_mem": gain_mem, "gain_dot": gain_dot, "out_weight": out_weight}


def feature_map(inputs):
    return jax.nn.elu(inputs) + 1.0

def head_norm(inputs, gain):
    return inputs * lax.rsqrt(lax.optimization_barrier(jnp.mean(inputs * inputs, axis=-1, keepdims=True)) + 1e-06) * gain

def reference(queries, keys, values, gain_mem, gain_dot, out_weight):
    number_of_segments = TOTAL_TOKENS // SEGMENT_TOKENS
    query_group_width = QUERY_HEADS // KEY_VALUE_HEADS
    highest = lax.Precision.HIGHEST
    segment_key_tiles = keys.reshape(number_of_segments, SEGMENT_TOKENS, KEY_VALUE_HEADS, HEAD_DIMENSION)
    segment_value_tiles = values.reshape(number_of_segments, SEGMENT_TOKENS, KEY_VALUE_HEADS, HEAD_DIMENSION)
    sig_keys = feature_map(segment_key_tiles.astype(jnp.float32)).astype(jnp.bfloat16)
    parts = jnp.einsum('sthd,sthe->shde', sig_keys.astype(jnp.float32), segment_value_tiles.astype(jnp.float32), precision=highest)
    running = jnp.cumsum(parts, axis=0)
    earlier = jnp.concatenate([jnp.zeros_like(parts[:1]), running[:-1]], axis=0)
    segment_query_tiles = queries.reshape(number_of_segments, SEGMENT_TOKENS, KEY_VALUE_HEADS, query_group_width, HEAD_DIMENSION)
    gain_memory = gain_mem.reshape(QUERY_HEADS, HEAD_DIMENSION)
    gain_attend = gain_dot.reshape(QUERY_HEADS, HEAD_DIMENSION)
    positions = jnp.arange(SEGMENT_TOKENS, dtype=jnp.int32)
    causal = positions[:, None] >= positions[None, :]
    scale = float(HEAD_DIMENSION) ** (-0.5)

    def per_segment(segment_items):
        query_block, key_block, value_block, memory = segment_items
        scores = jnp.einsum('rgjd,cgd->gjrc', query_block.astype(jnp.float32), key_block.astype(jnp.float32), precision=highest) * scale
        scores = jnp.where(causal, scores, -jnp.inf)
        row_max = lax.optimization_barrier(jnp.max(scores, axis=-1, keepdims=True))
        weights = jnp.where(causal, jnp.exp(scores - row_max), 0.0)
        denominator = lax.optimization_barrier(jnp.sum(weights, axis=-1, keepdims=True))
        weighted = jnp.einsum('gjrc,cgd->gjrd', weights.astype(jnp.bfloat16).astype(jnp.float32), value_block.astype(jnp.float32), precision=highest)
        dot_part = jnp.transpose(weighted / denominator, (2, 0, 1, 3)).reshape(SEGMENT_TOKENS, QUERY_HEADS, HEAD_DIMENSION)
        sig_queries = feature_map(query_block.astype(jnp.float32))
        memory_part = jnp.einsum('rgjd,gde->rgje', sig_queries, memory, precision=highest).reshape(SEGMENT_TOKENS, QUERY_HEADS, HEAD_DIMENSION)
        mixed = (0.5 * (head_norm(memory_part, gain_memory) + head_norm(dot_part, gain_attend))).astype(jnp.bfloat16)
        mixed = mixed.reshape(SEGMENT_TOKENS, QUERY_HEADS * HEAD_DIMENSION)
        return jnp.dot(mixed, out_weight, preferred_element_type=jnp.float32).astype(jnp.bfloat16)
    outputs = lax.map(per_segment, (segment_query_tiles, segment_key_tiles, segment_value_tiles, earlier))
    return outputs.reshape(TOTAL_TOKENS, QUERY_HEADS * HEAD_DIMENSION)
```

```python
import functools

import jax
import jax.numpy as jnp
from jax import lax
from jax.experimental import pallas as pl
from jax.experimental.pallas import tpu as pltpu
from jax.sharding import Mesh
from jax.sharding import PartitionSpec as P

HEAD = 128
GROUP = 4
AXES = ("sx", "sz", "y", "c")
EXP_SCALE = float(HEAD) ** (-0.5) * 1.4426950408889634
NT = (((1,), (1,)), ((), ()))
TN = (((0,), (0,)), ((), ()))
SMEM_SPEC = pl.BlockSpec(memory_space=pltpu.SMEM)


def feature_map(x):
    return jnp.where(x > 0, x + 1.0, jnp.exp(jnp.minimum(x, 0.0)))


def cost(flops, nbytes, trans=0):
    return pl.CostEstimate(flops=flops, bytes_accessed=nbytes, transcendentals=trans)


def prep_kv_kernel(pos, k, v, keep, send):
    half = k.shape[1] // 2
    for mine in range(2):

        @pl.when(pos[0] == mine)
        def _():
            a = slice(mine * half, (mine + 1) * half)
            b = slice((1 - mine) * half, (2 - mine) * half)
            keep[:, :half] = k[:, a]
            keep[:, half:] = v[:, a]
            send[:, :half] = k[:, b]
            send[:, half:] = v[:, b]


def prep_kv(pos, k, v):
    rows, cols = k.shape
    out = jax.ShapeDtypeStruct((rows, cols), k.dtype)
    vm = pl.BlockSpec(memory_space=pltpu.VMEM)
    return pl.pallas_call(
        prep_kv_kernel,
        out_shape=(out, out),
        in_specs=[SMEM_SPEC, vm, vm],
        out_specs=(vm, vm),
        name="prep_kv",
        cost_estimate=cost(0, 4 * rows * cols * 2),
    )(pos, k, v)


def prep_q_kernel(pos, q, keep, send):
    half = q.shape[1] // 2
    for mine in range(2):

        @pl.when(pos[0] == mine)
        def _():
            keep[...] = q[:, mine * half : (mine + 1) * half]
            send[...] = q[:, (1 - mine) * half : (2 - mine) * half]


def prep_q(pos, q):
    rows, cols = q.shape
    out = jax.ShapeDtypeStruct((rows, cols // 2), q.dtype)
    vm = pl.BlockSpec(memory_space=pltpu.VMEM)
    return pl.pallas_call(
        prep_q_kernel,
        out_shape=(out, out),
        in_specs=[SMEM_SPEC, vm],
        out_specs=(vm, vm),
        name="prep_q",
        cost_estimate=cost(0, 2 * rows * cols * 2),
    )(pos, q)


def part_kernel(pos, keep, recv, both, total):
    rows, cols = keep.shape
    heads = total.shape[0] // HEAD

    def put(first, second):
        both[:rows, :] = first[...]
        both[rows:, :] = second[...]

    pl.when(pos[0] == 0)(lambda: put(keep, recv))
    pl.when(pos[0] == 1)(lambda: put(recv, keep))
    for g in range(heads):
        kk = slice(g * HEAD, (g + 1) * HEAD)
        vv = slice(cols // 2 + g * HEAD, cols // 2 + (g + 1) * HEAD)
        acc = None
        for ref in (keep, recv):
            sig = feature_map(ref[:, kk].astype(jnp.float32)).astype(jnp.bfloat16)
            term = lax.dot_general(sig, ref[:, vv], TN, preferred_element_type=jnp.float32)
            acc = term if acc is None else acc + term
        total[kk, :] = acc


def part(pos, keep, recv):
    rows, cols = keep.shape
    vm = pl.BlockSpec(memory_space=pltpu.VMEM)
    return pl.pallas_call(
        part_kernel,
        out_shape=(
            jax.ShapeDtypeStruct((2 * rows, cols), keep.dtype),
            jax.ShapeDtypeStruct((cols // 2, HEAD), jnp.float32),
        ),
        in_specs=[SMEM_SPEC, vm, vm],
        out_specs=(vm, vm),
        name="part",
        cost_estimate=cost(4 * rows * cols // 2 * HEAD, 4 * rows * cols * 2),
    )(pos, keep, recv)


def attend_tile(q, k, v_ones, mask):
    s = lax.dot_general(q, k, NT, preferred_element_type=jnp.float32)
    if mask is not None:
        s = jnp.where(mask, s, -1e30)
    m = jnp.max(s, axis=-1, keepdims=True)
    return s, m


def weigh(s, m, v_ones):
    w = jnp.exp2(s * EXP_SCALE - m * EXP_SCALE).astype(jnp.bfloat16)
    return jnp.dot(w, v_ones, preferred_element_type=jnp.float32)


def with_ones(v):
    return jnp.concatenate([v, jnp.ones_like(v)], axis=1)


def first_kernel(pos, q_keep, q_recv, k, v, acc, stat):
    rows = q_keep.shape[0]
    keys = k.shape[0]
    v_ones = with_ones(v[...])
    for b, q in enumerate((q_keep, q_recv)):
        mine = pos[0] if b == 0 else 1 - pos[0]
        row = lax.broadcasted_iota(jnp.int32, (rows, keys), 0) + mine * rows
        mask = row >= lax.broadcasted_iota(jnp.int32, (rows, keys), 1)
        for j in range(GROUP):
            cols = slice(j * HEAD, (j + 1) * HEAD)
            s, m = attend_tile(q[:, cols], k[...], v_ones, mask)
            out = weigh(s, m, v_ones)
            acc[b, :, cols] = out[:, :HEAD]
            stat[b, :, j : j + 1] = m
            stat[b, :, GROUP + j : GROUP + j + 1] = out[:, HEAD : HEAD + 1]


def attn_specs(rows, keys):
    q_spec = pl.BlockSpec((rows, GROUP * HEAD), lambda g: (0, g))
    k_spec = pl.BlockSpec((keys, HEAD), lambda g: (0, g))
    v_spec = pl.BlockSpec((keys, HEAD), lambda g: (0, 2 + g))
    acc_spec = pl.BlockSpec((2, rows, GROUP * HEAD), lambda g: (0, 0, g))
    stat_spec = pl.BlockSpec((2, rows, HEAD), lambda g: (0, 0, g))
    return q_spec, k_spec, v_spec, acc_spec, stat_spec


def attend_cost(rows, keys, chunks):
    scores = 16 * rows * keys * chunks
    return cost(4 * scores * HEAD, 4 * 2**20, scores)


def attend_first(pos, q_keep, q_recv, kv):
    rows, keys = q_keep.shape[0], kv.shape[0]
    q_spec, k_spec, v_spec, acc_spec, stat_spec = attn_specs(rows, keys)
    return pl.pallas_call(
        first_kernel,
        grid=(2,),
        out_shape=(
            jax.ShapeDtypeStruct((2, rows, 2 * GROUP * HEAD), jnp.float32),
            jax.ShapeDtypeStruct((2, rows, 2 * HEAD), jnp.float32),
        ),
        in_specs=[SMEM_SPEC, q_spec, q_spec, k_spec, v_spec],
        out_specs=(acc_spec, stat_spec),
        name="attend_first",
        cost_estimate=attend_cost(rows, keys, 1),
    )(pos, q_keep, q_recv, kv, kv)


def fold_chunk(q_refs, k, v, acc, stat):
    v_ones = with_ones(v[...])
    for b, q in enumerate(q_refs):
        for j in range(GROUP):
            cols = slice(j * HEAD, (j + 1) * HEAD)
            s, m = attend_tile(q[:, cols], k[...], v_ones, None)
            old = stat[b, :, j : j + 1]
            new = jnp.maximum(old, m)
            out = weigh(s, new, v_ones)
            alpha = jnp.exp2(old * EXP_SCALE - new * EXP_SCALE)
            acc[b, :, cols] = acc[b, :, cols] * alpha + out[:, :HEAD]
            stat[b, :, j : j + 1] = new
            lane = slice(GROUP + j, GROUP + j + 1)
            stat[b, :, lane] = stat[b, :, lane] * alpha + out[:, HEAD : HEAD + 1]


def next_kernel(pos, q_keep, q_recv, k1, v1, k2, v2, acc_in, stat_in, acc, stat):
    acc[...] = acc_in[...]
    stat[...] = stat_in[...]
    fold = functools.partial(fold_chunk, (q_keep, q_recv))
    pl.when(pos[1] >= 1)(lambda: fold(k1, v1, acc, stat))
    pl.when(pos[1] == 3)(lambda: fold(k2, v2, acc, stat))


def attend_next(pos, q_keep, q_recv, left, right, acc, stat):
    rows, keys = q_keep.shape[0], left.shape[0]
    q_spec, k_spec, v_spec, acc_spec, stat_spec = attn_specs(rows, keys)
    return pl.pallas_call(
        next_kernel,
        grid=(2,),
        out_shape=(
            jax.ShapeDtypeStruct(acc.shape, acc.dtype),
            jax.ShapeDtypeStruct(stat.shape, stat.dtype),
        ),
        in_specs=[SMEM_SPEC, q_spec, q_spec, k_spec, v_spec, k_spec, v_spec, acc_spec, stat_spec],
        out_specs=(acc_spec, stat_spec),
        name="attend_next",
        cost_estimate=attend_cost(rows, keys, 2),
    )(pos, q_keep, q_recv, left, left, right, right, acc, stat)


def head_norm(x, gain):
    return x * lax.rsqrt(jnp.mean(x * x, axis=-1, keepdims=True) + 1e-06) * gain


def last_kernel(pos, q_keep, q_recv, k, v, acc_in, stat_in, m0, m1, m2, m3, gm, gd, keep, send, acc, stat):
    acc[...] = acc_in[...]
    stat[...] = stat_in[...]
    pl.when(pos[1] >= 2)(lambda: fold_chunk((q_keep, q_recv), k, v, acc, stat))
    memory = m0[...].astype(jnp.float32) + m1[...].astype(jnp.float32)
    memory = memory + m2[...].astype(jnp.float32) + m3[...].astype(jnp.float32)
    memory = memory.astype(jnp.bfloat16)
    for b, (q, out) in enumerate(((q_keep, keep), (q_recv, send))):
        for j in range(GROUP):
            cols = slice(j * HEAD, (j + 1) * HEAD)
            sig = feature_map(q[:, cols].astype(jnp.float32)).astype(jnp.bfloat16)
            read = jnp.dot(sig, memory, preferred_element_type=jnp.float32)
            dot = acc[b, :, cols] * (1.0 / stat[b, :, GROUP + j : GROUP + j + 1])
            mixed = head_norm(read, gm[:, cols]) + head_norm(dot, gd[:, cols])
            out[:, cols] = (0.5 * mixed).astype(jnp.bfloat16)


def attend_last(pos, q_keep, q_recv, far, acc, stat, memory, gain_mem, gain_dot):
    rows, keys = q_keep.shape[0], far.shape[0]
    q_spec, k_spec, v_spec, acc_spec, stat_spec = attn_specs(rows, keys)
    m_spec = pl.BlockSpec((HEAD, HEAD), lambda g: (g, 0))
    grid_spec = pltpu.PrefetchScalarGridSpec(
        num_scalar_prefetch=1,
        grid=(2,),
        in_specs=[
            pl.BlockSpec((rows, GROUP * HEAD), lambda g, p: (0, g)),
            pl.BlockSpec((rows, GROUP * HEAD), lambda g, p: (0, g)),
            pl.BlockSpec((keys, HEAD), lambda g, p: (0, g)),
            pl.BlockSpec((keys, HEAD), lambda g, p: (0, 2 + g)),
            pl.BlockSpec((2, rows, GROUP * HEAD), lambda g, p: (0, 0, g)),
            pl.BlockSpec((2, rows, HEAD), lambda g, p: (0, 0, g)),
        ]
        + [pl.BlockSpec((HEAD, HEAD), lambda g, p: (g, 0))] * 4
        + [pl.BlockSpec((1, GROUP * HEAD), lambda g, p: (0, 2 * p[0] + g))] * 2,
        out_specs=[pl.BlockSpec((rows, GROUP * HEAD), lambda g, p: (0, g))] * 2,
        scratch_shapes=[
            pltpu.VMEM((2, rows, GROUP * HEAD), jnp.float32),
            pltpu.VMEM((2, rows, HEAD), jnp.float32),
        ],
    )
    out = jax.ShapeDtypeStruct((rows, 2 * GROUP * HEAD), jnp.bfloat16)
    return pl.pallas_call(
        last_kernel,
        grid_spec=grid_spec,
        out_shape=(out, out),
        name="attend_last",
        cost_estimate=attend_cost(rows, keys, 1),
    )(pos, q_keep, q_recv, far, far, acc, stat, *memory, gain_mem, gain_dot)


def project_kernel(keep, recv, wa, wb, out):
    total = jnp.dot(keep[...], wa[...], preferred_element_type=jnp.float32)
    total = total + jnp.dot(recv[...], wb[...], preferred_element_type=jnp.float32)
    out[...] = total.astype(out.dtype)


def project(pos, keep, recv, weight):
    rows, inner = keep.shape
    width = weight.shape[1]
    tile = 256

    def kernel(p, *refs):
        project_kernel(*refs)

    grid_spec = pltpu.PrefetchScalarGridSpec(
        num_scalar_prefetch=1,
        grid=(width // tile,),
        in_specs=[
            pl.BlockSpec((rows, inner), lambda n, p: (0, 0)),
            pl.BlockSpec((rows, inner), lambda n, p: (0, 0)),
            pl.BlockSpec((inner, tile), lambda n, p: (p[0], n)),
            pl.BlockSpec((inner, tile), lambda n, p: (1 - p[0], n)),
        ],
        out_specs=pl.BlockSpec((rows, tile), lambda n, p: (0, n)),
    )
    return pl.pallas_call(
        kernel,
        grid_spec=grid_spec,
        out_shape=jax.ShapeDtypeStruct((rows, width), jnp.bfloat16),
        name="project",
        cost_estimate=cost(4 * rows * inner * width, 2 * inner * width * 2),
    )(pos, keep, recv, weight, weight)


def shift(x, axis, step, size):
    return lax.ppermute(x, axis, [(i, (i + step) % size) for i in range(size)])


def swap(x):
    return lax.ppermute(x, "c", [(0, 1), (1, 0)])


def earlier_memory(total, x, z):
    bf16 = jnp.bfloat16
    f32 = jnp.float32
    before = jnp.zeros_like(total)
    pairs = ([i ^ 1 for i in range(8)], [i ^ 2 for i in range(8)], [7 - i for i in range(8)])
    for level, partner in enumerate(pairs):
        got = lax.ppermute(total.astype(bf16), "sz", list(enumerate(partner))).astype(f32)
        upper = ((z >> level) & 1) == 1
        before = before + jnp.where(upper, got, 0.0)
        total = total + got
    sent = total.astype(bf16)
    for step in (1, 3, 2):
        got = shift(sent, "sx", step, 4).astype(f32)
        before = before + jnp.where(x >= step, got, 0.0)
    return before.astype(bf16)


def local(queries, keys, values, gain_mem, gain_dot, out_weight):
    x, z = lax.axis_index("sx"), lax.axis_index("sz")
    y, c = lax.axis_index("y"), lax.axis_index("c")
    pos = jnp.stack([c, y]).astype(jnp.int32)
    kv_keep, kv_send = prep_kv(pos, keys, values)
    kv_recv = swap(kv_send)
    q_keep, q_send = prep_q(pos, queries)
    q_recv = swap(q_send)
    kv, total = part(pos, kv_keep, kv_recv)
    left = shift(kv, "y", 1, 4)
    right = shift(kv, "y", 3, 4)
    far = shift(kv, "y", 2, 4)
    mine = earlier_memory(total, x, z)
    memory = (mine, shift(mine, "y", 1, 4), shift(mine, "y", 3, 4), shift(mine, "y", 2, 4))
    acc, stat = attend_first(pos, q_keep, q_recv, kv)
    acc, stat = attend_next(pos, q_keep, q_recv, left, right, acc, stat)
    mixed_keep, mixed_send = attend_last(
        pos, q_keep, q_recv, far, acc, stat, memory, gain_mem[None, :], gain_dot[None, :]
    )
    mixed_recv = swap(mixed_send)
    return project(pos, mixed_keep, mixed_recv, out_weight)


def solution(mesh):
    finer = Mesh(mesh.devices.reshape(4, 8, 4, 2), AXES)
    in_specs = (P(AXES, None), P(AXES, None), P(AXES, None), P(), P(), P())
    return jax.shard_map(
        local, mesh=finer, in_specs=in_specs, out_specs=P(AXES, None), check_vma=False
    )
```

```python
import functools

import jax
import jax.numpy as jnp
from jax import lax
from jax.experimental import pallas as pl
from jax.experimental.pallas import tpu as pltpu
from jax.sharding import Mesh
from jax.sharding import PartitionSpec as P


HEAD = 128
GROUP = 4
HEADS = 8
AXES = ("sx", "sz", "y", "c")
EXP_SCALE = float(HEAD) ** (-0.5) * 1.4426950408889634
NT = (((1,), (1,)), ((), ()))
TN = (((0,), (0,)), ((), ()))
BF16 = jnp.bfloat16
F32 = jnp.float32
VM = pl.BlockSpec(memory_space=pltpu.VMEM)
HBM = pl.BlockSpec(memory_space=pltpu.HBM)


def placed(x, space=pltpu.VMEM):
    return pltpu.with_memory_space_constraint(x, space)


def kernel_call(body, outs, args, limit, flops=0, nbytes=0, trans=0, specs=None, **more):
    specs = specs or [VM] * len(args)
    args = [placed(a, s.memory_space) for a, s in zip(args, specs)]
    return pl.pallas_call(
        body,
        out_shape=[pltpu.VMEM(shape, dtype) for shape, dtype in outs],
        in_specs=specs,
        out_specs=[VM] * len(outs),
        compiler_params=pltpu.CompilerParams(vmem_limit_bytes=limit * 2**20),
        cost_estimate=pl.CostEstimate(flops=flops, bytes_accessed=nbytes, transcendentals=trans),
        **more,
    )(*args)


def feature_map(x):
    return jnp.where(x > 0, x + 1.0, jnp.exp(jnp.minimum(x, 0.0)))


def prep_kv_kernel(k, v, keep, send, sems):
    half = k.shape[1] // 2
    c = lax.axis_index("c")
    copies = []
    for n, (out, who) in enumerate(((send, 1 - c), (keep, c))):
        cols = pl.ds(pl.multiple_of(who * half, half), half)
        for i, src in enumerate((k, v)):
            dst = out.at[:, i * half : (i + 1) * half]
            copies.append(pltpu.make_async_copy(src.at[:, cols], dst, sems.at[2 * n + i]))
    for copy in copies:
        copy.start()
    for copy in copies:
        copy.wait()


def prep_kv(k, v):
    outs = [(k.shape, BF16)] * 2
    return kernel_call(
        prep_kv_kernel, outs, (k, v), 8, nbytes=2**20, specs=[HBM, HBM],
        scratch_shapes=[pltpu.SemaphoreType.DMA((4,))],
    )


def prep_q_kernel(q, keep, send, sems):
    half = q.shape[1] // 2
    c = lax.axis_index("c")
    copies = []
    for n, (out, who) in enumerate(((send, 1 - c), (keep, c))):
        cols = pl.ds(pl.multiple_of(who * half, half), half)
        copies.append(pltpu.make_async_copy(q.at[:, cols], out, sems.at[n]))
    for copy in copies:
        copy.start()
    for copy in copies:
        copy.wait()


def prep_q(q):
    outs = [((q.shape[0], q.shape[1] // 2), BF16)] * 2
    return kernel_call(
        prep_q_kernel, outs, (q,), 8, nbytes=2**21, specs=[HBM],
        scratch_shapes=[pltpu.SemaphoreType.DMA((2,))],
    )


def part_kernel(keep, recv, both, total, sent):
    rows, cols = keep.shape
    mine = lax.axis_index("c") * rows
    other = rows - mine
    both[pl.ds(pl.multiple_of(mine, rows), rows), :] = keep[...]
    both[pl.ds(pl.multiple_of(other, rows), rows), :] = recv[...]
    for g in range(2):
        kk = slice(g * HEAD, (g + 1) * HEAD)
        vv = slice(cols // 2 + g * HEAD, cols // 2 + (g + 1) * HEAD)
        acc = None
        for ref in (keep, recv):
            sig = feature_map(ref[:, kk].astype(F32)).astype(BF16)
            term = lax.dot_general(sig, ref[:, vv], TN, preferred_element_type=F32)
            acc = term if acc is None else acc + term
        total[kk, :] = acc
        sent[kk, :] = acc.astype(BF16)


def part(keep, recv):
    rows, cols = keep.shape
    outs = [((2 * rows, cols), BF16), ((cols // 2, HEAD), F32), ((cols // 2, HEAD), BF16)]
    return kernel_call(part_kernel, outs, (keep, recv), 8, 2**26, 2**21)


def tiles():
    for g in range(2):
        for b in range(2):
            for j in range(GROUP):
                h = g * GROUP + j
                yield g, b, h, slice(h * HEAD, (h + 1) * HEAD), slice(2 * h * HEAD, 2 * (h + 1) * HEAD)


def fill_ones(kv, v_ones):
    for g in range(2):
        v = kv[:, (2 + g) * HEAD : (3 + g) * HEAD]
        v_ones[g] = jnp.concatenate([v, jnp.ones_like(v)], axis=1)


def weigh(s, m, v_ones):
    w = jnp.exp2(s * EXP_SCALE - m * EXP_SCALE).astype(BF16)
    return jnp.dot(w, v_ones, preferred_element_type=F32)


def first_kernel(q_keep, q_recv, kv, ext, top, v_ones):
    rows, keys = q_keep.shape[0], kv.shape[0]
    fill_ones(kv, v_ones)
    c = lax.axis_index("c")
    for g, b, h, cols, wide in tiles():
        q = (q_keep, q_recv)[b]
        first = (c if b == 0 else 1 - c) * rows
        row = lax.broadcasted_iota(jnp.int32, (rows, keys), 0) + first
        mask = row >= lax.broadcasted_iota(jnp.int32, (rows, keys), 1)
        s = lax.dot_general(
            q[:, cols], kv[:, g * HEAD : (g + 1) * HEAD], NT, preferred_element_type=F32
        )
        s = jnp.where(mask, s, -1e30)
        m = jnp.max(s, axis=-1, keepdims=True)
        ext[b, :, wide] = weigh(s, m, v_ones[g])
        top[b, :, cols] = jnp.broadcast_to(m, (rows, HEAD))


def state(rows):
    return [((2, rows, 2 * HEADS * HEAD), F32), ((2, rows, HEADS * HEAD), F32)]


def attend_first(q_keep, q_recv, kv):
    rows, keys = q_keep.shape[0], kv.shape[0]
    scores = 2 * HEADS * rows * keys
    return kernel_call(
        first_kernel, state(rows), (q_keep, q_recv, kv), 20,
        4 * scores * HEAD, 2**22, scores,
        scratch_shapes=[pltpu.VMEM((2, keys, 2 * HEAD), BF16)],
    )


def fold_chunk(q_refs, kv, v_ones, ext, top):
    keys = kv.shape[0]
    fill_ones(kv, v_ones)
    for g, b, h, cols, wide in tiles():
        s = lax.dot_general(
            q_refs[b][:, cols], kv[:, g * HEAD : (g + 1) * HEAD], NT, preferred_element_type=F32
        )
        old = top[b, :, cols]
        new = jnp.maximum(old, jnp.max(s, axis=-1, keepdims=True))
        floor = new * EXP_SCALE
        w = [
            jnp.exp2(s[:, n : n + HEAD] * EXP_SCALE - floor).astype(BF16)
            for n in range(0, keys, HEAD)
        ]
        out = jnp.dot(jnp.concatenate(w, axis=1), v_ones[g], preferred_element_type=F32)
        alpha = jnp.exp2(old * EXP_SCALE - floor)
        yield b, h, cols, wide, new, ext[b, :, wide] * jnp.concatenate([alpha, alpha], axis=1) + out


def next_kernel(q_keep, q_recv, left, right, ext_in, top_in, ext, top, v_ones):
    y = lax.axis_index("y")

    def fold(kv, source):
        for b, h, cols, wide, new, total in fold_chunk((q_keep, q_recv), kv, v_ones, *source):
            ext[b, :, wide] = total
            top[b, :, cols] = new

    pl.when(y >= 1)(lambda: fold(left, (ext, top)))
    pl.when(y == 3)(lambda: fold(right, (ext, top)))


def attend_next(q_keep, q_recv, left, right, ext, top):
    rows, keys = q_keep.shape[0], left.shape[0]
    scores = 2 * HEADS * rows * keys * 2
    return kernel_call(
        next_kernel, state(rows), (q_keep, q_recv, left, right, ext, top), 20,
        4 * scores * HEAD, 2**22, scores,
        scratch_shapes=[pltpu.VMEM((2, keys, 2 * HEAD), BF16)],
        input_output_aliases={4: 0, 5: 1},
    )


def head_norm(x, gain):
    return x * (0.5 * lax.rsqrt(jnp.mean(x * x, axis=-1, keepdims=True) + 1e-06)) * gain


def last_kernel(q_keep, q_recv, kv, ext, top, gain, out, v_ones):
    y, c = lax.axis_index("y"), lax.axis_index("c")
    own = pl.multiple_of(c * HEADS, HEADS)

    def put(b, h, cols, total):
        acc, den = total[:, :HEAD], total[:, HEAD:]
        square = jnp.mean(acc * acc + 1e-06 * (den * den), axis=-1, keepdims=True)
        out[b, :, cols] = acc * (0.5 * lax.rsqrt(square)) * gain[pl.ds(own + h, 1), :]

    @pl.when(y >= 2)
    def _():
        for b, h, cols, wide, new, total in fold_chunk((q_keep, q_recv), kv, v_ones, ext, top):
            put(b, h, cols, total)

    @pl.when(y < 2)
    def _():
        for g, b, h, cols, wide in tiles():
            put(b, h, cols, ext[b, :, wide])


def attend_last(q_keep, q_recv, far, ext, top, gain):
    rows, keys = q_keep.shape[0], far.shape[0]
    scores = 2 * HEADS * rows * keys
    outs = [((2, rows, HEADS * HEAD), F32)]
    return kernel_call(
        last_kernel, outs, (q_keep, q_recv, far, ext, top, gain), 20,
        4 * scores * HEAD, 2**22, scores,
        scratch_shapes=[pltpu.VMEM((2, keys, 2 * HEAD), BF16)],
    )[0]


def mix_kernel(q_keep, q_recv, dot, m0, m1, m2, m3, gain, keep, send):
    own = pl.multiple_of(lax.axis_index("c") * HEADS, HEADS)
    memory = (m0[...].astype(F32) + m1[...].astype(F32)) + (m2[...].astype(F32) + m3[...].astype(F32))
    memory = memory.astype(BF16)
    for g, b, h, cols, wide in tiles():
        q, out = ((q_keep, keep), (q_recv, send))[b]
        sig = feature_map(q[:, cols].astype(F32)).astype(BF16)
        read = jnp.dot(sig, memory[g * HEAD : (g + 1) * HEAD], preferred_element_type=F32)
        mixed = head_norm(read, gain[pl.ds(own + h, 1), :]) + dot[b, :, cols]
        out[:, cols] = mixed.astype(BF16)


def mix(q_keep, q_recv, dot, memory, gain):
    outs = [(q_keep.shape, BF16)] * 2
    args = (q_keep, q_recv, dot, *memory, gain)
    return kernel_call(mix_kernel, outs, args, 16, 2**27, 2**22)


def project_first_kernel(x, weight, out):
    half = x.shape[1]
    own = pl.multiple_of(lax.axis_index("c") * half, half)
    for n in range(0, weight.shape[1], 512):
        out[:, n : n + 512] = jnp.dot(
            x[...], weight[pl.ds(own, half), n : n + 512], preferred_element_type=F32
        )


def project_first(x, weight):
    outs = [((x.shape[0], weight.shape[1]), F32)]
    return kernel_call(project_first_kernel, outs, (x, weight), 16, 2**30, 2**23)[0]


def project_last_kernel(x, begun, weight, out):
    half = x.shape[1]
    other = pl.multiple_of(half - lax.axis_index("c") * half, half)
    n = pl.ds(pl.multiple_of(pl.program_id(0) * 512, 512), 512)
    total = begun[:, n] + jnp.dot(x[...], weight[pl.ds(other, half), n], preferred_element_type=F32)
    out[...] = total.astype(BF16)


def project_last(x, begun, weight):
    rows, width = begun.shape
    args = [placed(a) for a in (x, begun, weight)]
    return pl.pallas_call(
        project_last_kernel,
        grid=(width // 512,),
        out_shape=jax.ShapeDtypeStruct((rows, width), BF16),
        in_specs=[VM] * 3,
        out_specs=pl.BlockSpec((rows, 512), lambda n: (0, n)),
        name="project_last",
        compiler_params=pltpu.CompilerParams(vmem_limit_bytes=16 * 2**20),
        cost_estimate=pl.CostEstimate(flops=2**30, bytes_accessed=2**23, transcendentals=0),
    )(*args)


def permute(x, axis, partner):
    return lax.ppermute(x, axis, list(enumerate(partner)))


def shift(x, axis, step, size):
    return permute(x, axis, [(i + step) % size for i in range(size)])


def add_z_kernel(level, total, before, got, total_out, before_out, sent):
    upper = ((lax.axis_index("sz") >> level) & 1).astype(F32)
    term = got[...].astype(F32)
    before_out[...] = before[...] + term * upper
    total_out[...] = total[...] + term
    sent[...] = total_out[...].astype(BF16)


def add_x_kernel(before, x1, x2, x3, mine):
    x = lax.axis_index("sx")
    total = before[...]
    for step, ref in ((1, x1), (2, x2), (3, x3)):
        total = total + ref[...].astype(F32) * (x >= step).astype(F32)
    mine[...] = total.astype(BF16)


def earlier_memory(total, sent):
    before = jnp.zeros_like(total)
    pairs = ([i ^ 1 for i in range(8)], [i ^ 2 for i in range(8)], [7 - i for i in range(8)])
    outs = [(total.shape, F32), (total.shape, F32), (total.shape, BF16)]
    for level, partner in enumerate(pairs):
        got = permute(sent, "sz", partner)
        total, before, sent = kernel_call(
            functools.partial(add_z_kernel, level), outs, (total, before, got),
            4, 2**17, 2**18,
        )
    got = [shift(sent, "sx", step, 4) for step in (1, 2, 3)]
    return kernel_call(add_x_kernel, outs[2:], (before, *got), 4, 2**17, 2**18)[0]


def layer(queries, keys, values, gain_mem, gain_dot, out_weight):
    kv_keep, kv_send = prep_kv(keys, values)
    kv_recv = permute(kv_send, "c", (1, 0))
    q_keep, q_send = prep_q(queries)
    q_recv = permute(q_send, "c", (1, 0))
    kv, total, sent = part(kv_keep, kv_recv)
    left = shift(kv, "y", 1, 4)
    right = shift(kv, "y", 3, 4)
    far = shift(kv, "y", 2, 4)
    mine = earlier_memory(total, sent)
    memory = [mine] + [shift(mine, "y", step, 4) for step in (1, 2, 3)]
    ext, top = attend_first(q_keep, q_recv, kv)
    ext, top = attend_next(q_keep, q_recv, left, right, ext, top)
    gain_dot = gain_dot.reshape(2 * HEADS, HEAD)
    gain_mem = gain_mem.reshape(2 * HEADS, HEAD)
    dot = attend_last(q_keep, q_recv, far, ext, top, gain_dot)
    mixed_keep, mixed_send = mix(q_keep, q_recv, dot, memory, gain_mem)
    begun = project_first(mixed_keep, out_weight)
    mixed_recv = permute(mixed_send, "c", (1, 0))
    return project_last(mixed_recv, begun, out_weight)


def solution(mesh):
    finer = Mesh(mesh.devices.reshape(4, 8, 4, 2), AXES)
    in_specs = (P(AXES, None), P(AXES, None), P(AXES, None), P(), P(), P())
    return jax.shard_map(
        layer, mesh=finer, in_specs=in_specs, out_specs=P(AXES, None), check_vma=False
    )
```

```python
import functools

import jax
import jax.numpy as jnp
from jax import lax
from jax.experimental import pallas as pl
from jax.experimental.pallas import tpu as pltpu
from jax.sharding import Mesh
from jax.sharding import PartitionSpec as P


HEAD = 128
GROUP = 4
HEADS = 8
AXES = ("sx", "sz", "y", "c")
EXP_SCALE = float(HEAD) ** (-0.5) * 1.4426950408889634
NT = (((1,), (1,)), ((), ()))
TN = (((0,), (0,)), ((), ()))
BF16 = jnp.bfloat16
F32 = jnp.float32
VM = pl.BlockSpec(memory_space=pltpu.VMEM)
HBM = pl.BlockSpec(memory_space=pltpu.HBM)


def placed(x, space=pltpu.VMEM):
    return pltpu.with_memory_space_constraint(x, space)


def kernel_call(body, outs, args, limit, flops=0, nbytes=0, trans=0, specs=None, **more):
    specs = specs or [VM] * len(args)
    args = [placed(a, s.memory_space) for a, s in zip(args, specs)]
    return pl.pallas_call(
        body,
        out_shape=[pltpu.VMEM(shape, dtype) for shape, dtype in outs],
        in_specs=specs,
        out_specs=[VM] * len(outs),
        compiler_params=pltpu.CompilerParams(vmem_limit_bytes=limit * 2**20),
        cost_estimate=pl.CostEstimate(flops=flops, bytes_accessed=nbytes, transcendentals=trans),
        **more,
    )(*args)


def feature_map(x):
    return jnp.where(x > 0, x + 1.0, jnp.exp(jnp.minimum(x, 0.0)))


def prep_kernel(k, v, q, kv_own, q_own, sems):
    half = k.shape[1] // 2
    c = lax.axis_index("c")
    moves = [(k, kv_own.at[:, :half], half), (v, kv_own.at[:, half:], half), (q, q_own, 4 * half)]
    copies = []
    for n, (src, dst, width) in enumerate(moves):
        cols = pl.ds(pl.multiple_of(c * width, width), width)
        copies.append(pltpu.make_async_copy(src.at[:, cols], dst, sems.at[n]))
        copies[-1].start()
    for copy in copies:
        copy.wait()


def prep(k, v, q):
    outs = [(k.shape, BF16), ((q.shape[0], q.shape[1] // 2), BF16)]
    return kernel_call(
        prep_kernel, outs, (k, v, q), 8, nbytes=2**21, specs=[HBM] * 3,
        scratch_shapes=[pltpu.SemaphoreType.DMA((3,))],
    )


def part_kernel(kv_own, k_recv, v_recv, both, total, sent):
    rows, half = k_recv.shape[0], k_recv.shape[1] // 2
    c = lax.axis_index("c")
    own = pl.ds(pl.multiple_of(c * half, half), half)
    both[pl.ds(pl.multiple_of(c * rows, rows), rows), :] = kv_own[...]
    for i, ref in enumerate((k_recv, v_recv)):
        at = pl.ds(pl.multiple_of(rows - c * rows, rows), rows)
        both[at, i * half : (i + 1) * half] = ref[:, own]
    for g in range(2):
        kk = slice(g * HEAD, (g + 1) * HEAD)
        vv = slice(half + g * HEAD, half + (g + 1) * HEAD)
        sig = feature_map(both[:, kk].astype(F32)).astype(BF16)
        acc = lax.dot_general(sig, both[:, vv], TN, preferred_element_type=F32)
        total[kk, :] = acc
        sent[kk, :] = acc.astype(BF16)


def part(kv_own, k_recv, v_recv):
    rows, cols = kv_own.shape
    outs = [((2 * rows, cols), BF16), ((cols // 2, HEAD), F32), ((cols // 2, HEAD), BF16)]
    return kernel_call(part_kernel, outs, (kv_own, k_recv, v_recv), 8, 2**26, 2**21)


def tiles(rows=256, size=128):
    for g in range(2):
        for b in range(2):
            for j in range(GROUP):
                h = g * GROUP + j
                cols, wide = slice(h * HEAD, (h + 1) * HEAD), slice(2 * h * HEAD, 2 * (h + 1) * HEAD)
                for r in range(0, rows, size):
                    yield g, b, h, slice(r, r + size), cols, wide


def head_of(q, h):
    if q.shape[1] == HEADS * HEAD:
        return slice(h * HEAD, (h + 1) * HEAD)
    first = lax.axis_index("c") * (HEADS * HEAD) + h * HEAD
    return pl.ds(pl.multiple_of(first, HEAD), HEAD)


def fill_ones(kv, v_ones):
    for g in range(2):
        v = kv[:, (2 + g) * HEAD : (3 + g) * HEAD]
        v_ones[g] = jnp.concatenate([v, jnp.ones_like(v)], axis=1)


def scores(q_refs, kv, g, b, h, r):
    q, k = q_refs[b][r, head_of(q_refs[b], h)], kv[:, g * HEAD : (g + 1) * HEAD]
    return lax.dot_general(q, k, NT, preferred_element_type=F32)


def weigh(s, new, v_ones):
    w = [
        jnp.exp2((s[:, n : n + HEAD] - new) * EXP_SCALE).astype(BF16)
        for n in range(0, s.shape[1], HEAD)
    ]
    return jnp.dot(jnp.concatenate(w, axis=1), v_ones, preferred_element_type=F32)


def first_kernel(q_keep, q_recv, kv, ext, top, v_ones):
    rows = q_keep.shape[0]
    fill_ones(kv, v_ones)
    c = lax.axis_index("c")
    for g, b, h, r, cols, wide in tiles():
        s = scores((q_keep, q_recv), kv, g, b, h, r)
        first = (c if b == 0 else 1 - c) * rows + r.start
        row = lax.broadcasted_iota(jnp.int32, s.shape, 0) + first
        s = jnp.where(row >= lax.broadcasted_iota(jnp.int32, s.shape, 1), s, -1e30)
        m = jnp.broadcast_to(jnp.max(s, axis=-1, keepdims=True), (s.shape[0], HEAD))
        ext[b, r, wide] = weigh(s, m, v_ones[g])
        top[b, r, cols] = m


def state(rows):
    return [((2, rows, 2 * HEADS * HEAD), F32), ((2, rows, HEADS * HEAD), F32)]


def attend_first(q_keep, q_recv, kv):
    rows, keys = q_keep.shape[0], kv.shape[0]
    count = 2 * HEADS * rows * keys
    return kernel_call(
        first_kernel, state(rows), (q_keep, q_recv, kv), 20,
        4 * count * HEAD, 2**22, count,
        scratch_shapes=[pltpu.VMEM((2, keys, 2 * HEAD), BF16)],
    )


def fold_chunk(q_refs, kv, v_ones, ext, top):
    fill_ones(kv, v_ones)
    for g, b, h, r, cols, wide in tiles():
        s = scores(q_refs, kv, g, b, h, r)
        old = top[b, r, cols]
        new = jnp.maximum(old, jnp.max(s, axis=-1, keepdims=True))
        alpha = jnp.exp2((old - new) * EXP_SCALE)
        total = ext[b, r, wide] * jnp.concatenate([alpha, alpha], axis=1) + weigh(s, new, v_ones[g])
        yield b, h, r, cols, wide, new, total


def next_kernel(first_y, q_keep, q_recv, kv, ext_in, top_in, ext, top, v_ones):
    @pl.when(lax.axis_index("y") >= first_y)
    def _():
        for b, h, r, cols, wide, new, total in fold_chunk((q_keep, q_recv), kv, v_ones, ext, top):
            ext[b, r, wide] = total
            top[b, r, cols] = new


def attend_next(first_y, q_keep, q_recv, kv, ext, top):
    rows, keys = q_keep.shape[0], kv.shape[0]
    count = 2 * HEADS * rows * keys
    return kernel_call(
        functools.partial(next_kernel, first_y), state(rows), (q_keep, q_recv, kv, ext, top),
        20, 4 * count * HEAD, 2**22, count,
        scratch_shapes=[pltpu.VMEM((2, keys, 2 * HEAD), BF16)],
        input_output_aliases={3: 0, 4: 1},
    )


def head_norm(x, gain):
    return x * (0.5 * lax.rsqrt(jnp.mean(x * x, axis=-1, keepdims=True) + 1e-06)) * gain


def last_kernel(q_keep, q_recv, kv_a, kv_b, ext, top, gain, out, kv, v_ones):
    y, c = lax.axis_index("y"), lax.axis_index("c")
    own = pl.multiple_of(c * HEADS, HEADS)

    def put(b, h, r, cols, total):
        acc, den = total[:, :HEAD], total[:, HEAD:]
        square = jnp.mean(acc * acc + 1e-06 * (den * den), axis=-1, keepdims=True)
        out[b, r, cols] = acc * (0.5 * lax.rsqrt(square)) * gain[pl.ds(own + h, 1), :]

    @pl.when(y >= 2)
    def _():
        half = kv_a.shape[0]
        kv[:half, :] = kv_a[...]
        kv[half:, :] = kv_b[...]
        for b, h, r, cols, wide, new, total in fold_chunk((q_keep, q_recv), kv, v_ones, ext, top):
            put(b, h, r, cols, total)

    @pl.when(y < 2)
    def _():
        for g, b, h, r, cols, wide in tiles():
            put(b, h, r, cols, ext[b, r, wide])


def attend_last(q_keep, q_recv, far, ext, top, gain):
    rows, keys, width = q_keep.shape[0], 2 * far[0].shape[0], far[0].shape[1]
    count = 2 * HEADS * rows * keys
    outs = [((2, rows, HEADS * HEAD), F32)]
    return kernel_call(
        last_kernel, outs, (q_keep, q_recv, *far, ext, top, gain), 20,
        4 * count * HEAD, 2**22, count,
        scratch_shapes=[pltpu.VMEM((keys, width), BF16), pltpu.VMEM((2, keys, 2 * HEAD), BF16)],
    )[0]


def sig_kernel(q_keep, q_recv, sig):
    for b, q in enumerate((q_keep, q_recv)):
        for h in range(HEADS):
            x = q[:, head_of(q, h)].astype(F32)
            sig[b, :, h * HEAD : (h + 1) * HEAD] = feature_map(x).astype(BF16)


def mix_kernel(b, sig, dot, m0, m1, m2, m3, gain, out):
    own = pl.multiple_of(lax.axis_index("c") * HEADS, HEADS)
    memory = (m0[...].astype(F32) + m1[...].astype(F32)) + (m2[...].astype(F32) + m3[...].astype(F32))
    memory = memory.astype(BF16)
    for h in range(HEADS):
        cols, g = slice(h * HEAD, (h + 1) * HEAD), h // GROUP
        read = jnp.dot(
            sig[b, :, cols], memory[g * HEAD : (g + 1) * HEAD], preferred_element_type=F32
        )
        mixed = head_norm(read, gain[pl.ds(own + h, 1), :]) + dot[b, :, cols]
        out[:, cols] = mixed.astype(BF16)


def mix(b, sig, dot, memory, gain):
    outs = [(sig.shape[1:], BF16)]
    body = functools.partial(mix_kernel, b)
    return kernel_call(body, outs, (sig, dot, *memory, gain), 12, 2**26, 2**21)[0]


def project_first_kernel(x, weight, out):
    half = x.shape[1]
    own = pl.multiple_of(lax.axis_index("c") * half, half)
    for n in range(0, weight.shape[1], 512):
        out[:, n : n + 512] = jnp.dot(
            x[...], weight[pl.ds(own, half), n : n + 512], preferred_element_type=F32
        )


def project_first(x, weight):
    outs = [((x.shape[0], weight.shape[1]), F32)]
    return kernel_call(project_first_kernel, outs, (x, weight), 16, 2**30, 2**23)[0]


def project_last_kernel(x, begun, weight, out, stage, sems):
    half, width = x.shape[1], 256
    other = pl.multiple_of(half - lax.axis_index("c") * half, half)
    copies = []
    for i in range(out.shape[1] // width):
        n = slice(i * width, (i + 1) * width)
        total = jnp.dot(x[...], weight[pl.ds(other, half), n], preferred_element_type=F32)
        stage[:, n] = (begun[:, n] + total).astype(BF16)
        copies.append(pltpu.make_async_copy(stage.at[:, n], out.at[:, n], sems.at[i]))
        copies[-1].start()
    for copy in copies:
        copy.wait()


def project_last(x, begun, weight):
    shape = begun.shape
    return pl.pallas_call(
        project_last_kernel,
        out_shape=pltpu.HBM(shape, BF16),
        in_specs=[VM] * 3,
        out_specs=HBM,
        scratch_shapes=[pltpu.VMEM(shape, BF16), pltpu.SemaphoreType.DMA((shape[1] // 256,))],
        name="project_last",
        compiler_params=pltpu.CompilerParams(vmem_limit_bytes=16 * 2**20),
        cost_estimate=pl.CostEstimate(flops=2**30, bytes_accessed=2**23, transcendentals=0),
    )(*[placed(a) for a in (x, begun, weight)])


def permute(x, axis, partner):
    return lax.ppermute(x, axis, list(enumerate(partner)))


def shift(x, axis, step, size):
    return permute(x, axis, [(i + step) % size for i in range(size)])


def add_kernel(axis, level, total, before, got, before_out, *more):
    upper = ((lax.axis_index(axis) >> level) & 1).astype(F32)
    term = got[...].astype(F32)
    earlier = before[...] + term * upper
    before_out[...] = earlier.astype(before_out.dtype)
    if more:
        total_out, sent = more
        summed = total[...] + term
        total_out[...] = summed
        sent[...] = summed.astype(BF16)


def earlier_memory(total, sent):
    before = jnp.zeros_like(total)
    shape = total.shape
    steps = (
        ("sz", 0, [i ^ 1 for i in range(8)], "z1"),
        ("sz", 1, [i ^ 2 for i in range(8)], "z2"),
        ("sz", 2, [7 - i for i in range(8)], "z3"),
        ("sx", 0, [i ^ 1 for i in range(4)], "x1"),
        ("sx", 1, [i ^ 2 for i in range(4)], "x2"),
    )
    for axis, level, partner, name in steps:
        last = name == "x2"
        got = permute(sent, axis, partner)
        outs = [(shape, BF16)] if last else [(shape, F32), (shape, F32), (shape, BF16)]
        result = kernel_call(
            functools.partial(add_kernel, axis, level), outs, (total, before, got),
            4, 2**17, 2**18,
        )
        if last:
            return result[0]
        before, total, sent = result


def layer(queries, keys, values, gain_mem, gain_dot, out_weight):
    k_recv = permute(keys, "c", (1, 0))
    v_recv = permute(values, "c", (1, 0))
    q_recv = permute(queries, "c", (1, 0))
    kv_own, q_own = prep(keys, values, queries)
    kv, total, sent = part(kv_own, k_recv, v_recv)
    left = shift(kv, "y", 1, 4)
    right = shift(kv, "y", 3, 4)
    half = kv.shape[0] // 2
    far = shift(left[:half], "y", 1, 4), shift(right[half:], "y", 3, 4)
    mine = earlier_memory(total, sent)
    memory = [mine] + [shift(mine, "y", step, 4) for step in (1, 2, 3)]
    ext, top = attend_first(q_own, q_recv, kv)
    ext, top = attend_next(1, q_own, q_recv, left, ext, top)
    ext, top = attend_next(3, q_own, q_recv, right, ext, top)
    gain_dot = gain_dot.reshape(2 * HEADS, HEAD)
    gain_mem = gain_mem.reshape(2 * HEADS, HEAD)
    dot = attend_last(q_own, q_recv, far, ext, top, gain_dot)
    shape = (2, *q_own.shape)
    sig = kernel_call(sig_kernel, [(shape, BF16)], (q_own, q_recv), 8, 2**21, 2**22)[0]
    mixed_send = mix(1, sig, dot, memory, gain_mem)
    mixed_keep = mix(0, sig, dot, memory, gain_mem)
    begun = project_first(mixed_keep, out_weight)
    mixed_recv = permute(mixed_send, "c", (1, 0))
    return project_last(mixed_recv, begun, out_weight)


def solution(mesh):
    finer = Mesh(mesh.devices.reshape(4, 8, 4, 2), AXES)
    in_specs = (P(AXES, None), P(AXES, None), P(AXES, None), P(), P(), P())
    return jax.shard_map(
        layer, mesh=finer, in_specs=in_specs, out_specs=P(AXES, None), check_vma=False
    )
```

```python
import functools

import jax
import jax.numpy as jnp
from jax import lax
from jax.experimental import pallas as pl
from jax.experimental.pallas import tpu as pltpu
from jax.sharding import Mesh
from jax.sharding import PartitionSpec as P


HEAD = 128
GROUP = 4
HEADS = 8
AXES = ("sx", "sz", "y", "c")
EXP_SCALE = float(HEAD) ** (-0.5) * 1.4426950408889634
NT = (((1,), (1,)), ((), ()))
TN = (((0,), (0,)), ((), ()))
BF16 = jnp.bfloat16
F32 = jnp.float32
VM = pl.BlockSpec(memory_space=pltpu.VMEM)
HBM = pl.BlockSpec(memory_space=pltpu.HBM)


def placed(x, space=pltpu.VMEM):
    return pltpu.with_memory_space_constraint(x, space)


def kernel_call(body, outs, args, limit, flops=0, nbytes=0, trans=0, specs=None, **more):
    specs = specs or [VM] * len(args)
    args = [placed(a, s.memory_space) for a, s in zip(args, specs)]
    return pl.pallas_call(
        body,
        out_shape=[pltpu.VMEM(shape, dtype) for shape, dtype in outs],
        in_specs=specs,
        out_specs=[VM] * len(outs),
        compiler_params=pltpu.CompilerParams(vmem_limit_bytes=limit * 2**20),
        cost_estimate=pl.CostEstimate(flops=flops, bytes_accessed=nbytes, transcendentals=trans),
        **more,
    )(*args)


def feature_map(x):
    return jnp.where(x > 0, x + 1.0, jnp.exp(jnp.minimum(x, 0.0)))


def prep_kernel(k, v, q, kv_own, q_own, sems):
    half = k.shape[1] // 2
    c = lax.axis_index("c")
    moves = [(k, kv_own.at[:, :half], half), (v, kv_own.at[:, half:], half), (q, q_own, 4 * half)]
    copies = []
    for n, (src, dst, width) in enumerate(moves):
        cols = pl.ds(pl.multiple_of(c * width, width), width)
        copies.append(pltpu.make_async_copy(src.at[:, cols], dst, sems.at[n]))
        copies[-1].start()
    for copy in copies:
        copy.wait()


def prep(k, v, q):
    outs = [(k.shape, BF16), ((q.shape[0], q.shape[1] // 2), BF16)]
    return kernel_call(
        prep_kernel, outs, (k, v, q), 8, nbytes=2**21, specs=[HBM] * 3,
        scratch_shapes=[pltpu.SemaphoreType.DMA((3,))],
    )


def part_kernel(kv_own, k_recv, v_recv, both, total, sent):
    rows, half = k_recv.shape[0], k_recv.shape[1] // 2
    c = lax.axis_index("c")
    own = pl.ds(pl.multiple_of(c * half, half), half)
    both[pl.ds(pl.multiple_of(c * rows, rows), rows), :] = kv_own[...]
    for i, ref in enumerate((k_recv, v_recv)):
        at = pl.ds(pl.multiple_of(rows - c * rows, rows), rows)
        both[at, i * half : (i + 1) * half] = ref[:, own]
    for g in range(2):
        kk = slice(g * HEAD, (g + 1) * HEAD)
        vv = slice(half + g * HEAD, half + (g + 1) * HEAD)
        sig = feature_map(both[:, kk].astype(F32)).astype(BF16)
        acc = lax.dot_general(sig, both[:, vv], TN, preferred_element_type=F32)
        total[kk, :] = acc
        sent[kk, :] = acc.astype(BF16)


def part(kv_own, k_recv, v_recv):
    rows, cols = kv_own.shape
    outs = [((2 * rows, cols), BF16), ((cols // 2, HEAD), F32), ((cols // 2, HEAD), BF16)]
    return kernel_call(part_kernel, outs, (kv_own, k_recv, v_recv), 8, 2**26, 2**21)


def tiles(rows=256, size=128):
    for g in range(2):
        for b in range(2):
            for j in range(GROUP):
                h = g * GROUP + j
                cols, wide = slice(h * HEAD, (h + 1) * HEAD), slice(2 * h * HEAD, 2 * (h + 1) * HEAD)
                for r in range(0, rows, size):
                    yield g, b, h, slice(r, r + size), cols, wide


def head_of(q, h):
    if q.shape[1] == HEADS * HEAD:
        return slice(h * HEAD, (h + 1) * HEAD)
    first = lax.axis_index("c") * (HEADS * HEAD) + h * HEAD
    return pl.ds(pl.multiple_of(first, HEAD), HEAD)


def fill_ones(kv, v_ones):
    for g in range(2):
        v = kv[:, (2 + g) * HEAD : (3 + g) * HEAD]
        v_ones[g] = jnp.concatenate([v, jnp.ones_like(v)], axis=1)


def scores(q_refs, kv, g, b, h, r):
    q, k = q_refs[b][r, head_of(q_refs[b], h)], kv[:, g * HEAD : (g + 1) * HEAD]
    return lax.dot_general(q, k, NT, preferred_element_type=F32)


def weigh(s, new, v_ones):
    w = [
        jnp.exp2((s[:, n : n + HEAD] - new) * EXP_SCALE).astype(BF16)
        for n in range(0, s.shape[1], HEAD)
    ]
    return jnp.dot(jnp.concatenate(w, axis=1), v_ones, preferred_element_type=F32)


def first_kernel(q_keep, q_recv, kv, ext, top, v_ones):
    rows = q_keep.shape[0]
    fill_ones(kv, v_ones)
    c = lax.axis_index("c")
    for g, b, h, r, cols, wide in tiles():
        s = scores((q_keep, q_recv), kv, g, b, h, r)
        first = (c if b == 0 else 1 - c) * rows + r.start
        row = lax.broadcasted_iota(jnp.int32, s.shape, 0) + first
        s = jnp.where(row >= lax.broadcasted_iota(jnp.int32, s.shape, 1), s, -1e30)
        m = jnp.broadcast_to(jnp.max(s, axis=-1, keepdims=True), (s.shape[0], HEAD))
        ext[b, r, wide] = weigh(s, m, v_ones[g])
        top[b, r, cols] = m


def state(rows):
    return [((2, rows, 2 * HEADS * HEAD), F32), ((2, rows, HEADS * HEAD), F32)]


def attend_first(q_keep, q_recv, kv):
    rows, keys = q_keep.shape[0], kv.shape[0]
    count = 2 * HEADS * rows * keys
    return kernel_call(
        first_kernel, state(rows), (q_keep, q_recv, kv), 20,
        4 * count * HEAD, 2**22, count,
        scratch_shapes=[pltpu.VMEM((2, keys, 2 * HEAD), BF16)],
    )


def fold_chunk(q_refs, kv, v_ones, ext, top):
    fill_ones(kv, v_ones)
    for g, b, h, r, cols, wide in tiles():
        s = scores(q_refs, kv, g, b, h, r)
        old = top[b, r, cols]
        new = jnp.maximum(old, jnp.max(s, axis=-1, keepdims=True))
        alpha = jnp.exp2((old - new) * EXP_SCALE)
        total = ext[b, r, wide] * jnp.concatenate([alpha, alpha], axis=1) + weigh(s, new, v_ones[g])
        yield b, h, r, cols, wide, new, total


def next_kernel(first_y, q_keep, q_recv, kv, ext_in, top_in, ext, top, v_ones):
    @pl.when(lax.axis_index("y") >= first_y)
    def _():
        for b, h, r, cols, wide, new, total in fold_chunk((q_keep, q_recv), kv, v_ones, ext, top):
            ext[b, r, wide] = total
            top[b, r, cols] = new


def attend_next(first_y, q_keep, q_recv, kv, ext, top):
    rows, keys = q_keep.shape[0], kv.shape[0]
    count = 2 * HEADS * rows * keys
    return kernel_call(
        functools.partial(next_kernel, first_y), state(rows), (q_keep, q_recv, kv, ext, top),
        20, 4 * count * HEAD, 2**22, count,
        scratch_shapes=[pltpu.VMEM((2, keys, 2 * HEAD), BF16)],
        input_output_aliases={3: 0, 4: 1},
    )


def head_norm(x, gain):
    return x * (0.5 * lax.rsqrt(jnp.mean(x * x, axis=-1, keepdims=True) + 1e-06)) * gain


def last_kernel(q_keep, q_recv, kv, ext, top, gain, out, v_ones):
    y, c = lax.axis_index("y"), lax.axis_index("c")
    own = pl.multiple_of(c * HEADS, HEADS)

    def put(b, h, r, cols, total):
        acc, den = total[:, :HEAD], total[:, HEAD:]
        square = jnp.mean(acc * acc + 1e-06 * (den * den), axis=-1, keepdims=True)
        out[b, r, cols] = acc * (0.5 * lax.rsqrt(square)) * gain[pl.ds(own + h, 1), :]

    @pl.when(y >= 2)
    def _():
        for b, h, r, cols, wide, new, total in fold_chunk((q_keep, q_recv), kv, v_ones, ext, top):
            put(b, h, r, cols, total)

    @pl.when(y < 2)
    def _():
        for g, b, h, r, cols, wide in tiles():
            put(b, h, r, cols, ext[b, r, wide])


def attend_last(q_keep, q_recv, far, ext, top, gain):
    rows, keys = q_keep.shape[0], far.shape[0]
    count = 2 * HEADS * rows * keys
    outs = [((2, rows, HEADS * HEAD), F32)]
    return kernel_call(
        last_kernel, outs, (q_keep, q_recv, far, ext, top, gain), 20,
        4 * count * HEAD, 2**22, count,
        scratch_shapes=[pltpu.VMEM((2, keys, 2 * HEAD), BF16)],
    )[0]


def sig_kernel(q_keep, q_recv, sig):
    for b, q in enumerate((q_keep, q_recv)):
        for h in range(HEADS):
            x = q[:, head_of(q, h)].astype(F32)
            sig[b, :, h * HEAD : (h + 1) * HEAD] = feature_map(x).astype(BF16)


def mix_kernel(b, sig, dot, m0, m1, m2, m3, gain, out):
    own = pl.multiple_of(lax.axis_index("c") * HEADS, HEADS)
    memory = (m0[...].astype(F32) + m1[...].astype(F32)) + (m2[...].astype(F32) + m3[...].astype(F32))
    memory = memory.astype(BF16)
    for h in range(HEADS):
        cols, g = slice(h * HEAD, (h + 1) * HEAD), h // GROUP
        read = jnp.dot(
            sig[b, :, cols], memory[g * HEAD : (g + 1) * HEAD], preferred_element_type=F32
        )
        mixed = head_norm(read, gain[pl.ds(own + h, 1), :]) + dot[b, :, cols]
        out[:, cols] = mixed.astype(BF16)


def mix(b, sig, dot, memory, gain):
    outs = [(sig.shape[1:], BF16)]
    body = functools.partial(mix_kernel, b)
    return kernel_call(body, outs, (sig, dot, *memory, gain), 12, 2**26, 2**21)[0]


def project_first_kernel(x, weight, out):
    half = x.shape[1]
    own = pl.multiple_of(lax.axis_index("c") * half, half)
    for n in range(0, weight.shape[1], 512):
        out[:, n : n + 512] = jnp.dot(
            x[...], weight[pl.ds(own, half), n : n + 512], preferred_element_type=F32
        )


def project_first(x, weight):
    outs = [((x.shape[0], weight.shape[1]), F32)]
    return kernel_call(project_first_kernel, outs, (x, weight), 16, 2**30, 2**23)[0]


def project_last_kernel(x, begun, weight, out, stage, sems):
    half, width = x.shape[1], 256
    other = pl.multiple_of(half - lax.axis_index("c") * half, half)
    copies = []
    for i in range(out.shape[1] // width):
        n = slice(i * width, (i + 1) * width)
        total = jnp.dot(x[...], weight[pl.ds(other, half), n], preferred_element_type=F32)
        stage[:, n] = (begun[:, n] + total).astype(BF16)
        copies.append(pltpu.make_async_copy(stage.at[:, n], out.at[:, n], sems.at[i]))
        copies[-1].start()
    for copy in copies:
        copy.wait()


def project_last(x, begun, weight):
    shape = begun.shape
    return pl.pallas_call(
        project_last_kernel,
        out_shape=pltpu.HBM(shape, BF16),
        in_specs=[VM] * 3,
        out_specs=HBM,
        scratch_shapes=[pltpu.VMEM(shape, BF16), pltpu.SemaphoreType.DMA((shape[1] // 256,))],
        name="project_last",
        compiler_params=pltpu.CompilerParams(vmem_limit_bytes=16 * 2**20),
        cost_estimate=pl.CostEstimate(flops=2**30, bytes_accessed=2**23, transcendentals=0),
    )(*[placed(a) for a in (x, begun, weight)])


def permute(x, axis, partner):
    return lax.ppermute(x, axis, list(enumerate(partner)))


def shift(x, axis, step, size):
    return permute(x, axis, [(i + step) % size for i in range(size)])


def add_kernel(axis, level, total, before, got, before_out, *more):
    upper = ((lax.axis_index(axis) >> level) & 1).astype(F32)
    term = got[...].astype(F32)
    earlier = before[...] + term * upper
    before_out[...] = earlier.astype(before_out.dtype)
    if more:
        total_out, sent = more
        summed = total[...] + term
        total_out[...] = summed
        sent[...] = summed.astype(BF16)


def earlier_memory(total, sent):
    before = jnp.zeros_like(total)
    shape = total.shape
    steps = (
        ("sz", 0, [i ^ 1 for i in range(8)], "z1"),
        ("sz", 1, [i ^ 2 for i in range(8)], "z2"),
        ("sz", 2, [7 - i for i in range(8)], "z3"),
        ("sx", 0, [i ^ 1 for i in range(4)], "x1"),
        ("sx", 1, [3 - i for i in range(4)], "x2"),
    )
    for axis, level, partner, name in steps:
        last = name == "x2"
        got = permute(sent, axis, partner)
        outs = [(shape, BF16)] if last else [(shape, F32), (shape, F32), (shape, BF16)]
        result = kernel_call(
            functools.partial(add_kernel, axis, level), outs, (total, before, got),
            4, 2**17, 2**18,
        )
        if last:
            return result[0]
        before, total, sent = result


def layer(queries, keys, values, gain_mem, gain_dot, out_weight):
    k_recv = permute(keys, "c", (1, 0))
    v_recv = permute(values, "c", (1, 0))
    q_recv = permute(queries, "c", (1, 0))
    kv_own, q_own = prep(keys, values, queries)
    kv, total, sent = part(kv_own, k_recv, v_recv)
    left = shift(kv, "y", 1, 4)
    right = shift(kv, "y", 3, 4)
    far = permute(kv, "y", [i ^ 2 for i in range(4)])
    mine = earlier_memory(total, sent)
    memory = [mine] + [permute(mine, "y", [i ^ n for i in range(4)]) for n in (1, 2, 3)]
    ext, top = attend_first(q_own, q_recv, kv)
    ext, top = attend_next(1, q_own, q_recv, left, ext, top)
    ext, top = attend_next(3, q_own, q_recv, right, ext, top)
    gain_dot = gain_dot.reshape(2 * HEADS, HEAD)
    gain_mem = gain_mem.reshape(2 * HEADS, HEAD)
    dot = attend_last(q_own, q_recv, far, ext, top, gain_dot)
    shape = (2, *q_own.shape)
    sig = kernel_call(sig_kernel, [(shape, BF16)], (q_own, q_recv), 8, 2**21, 2**22)[0]
    mixed_send = mix(1, sig, dot, memory, gain_mem)
    mixed_keep = mix(0, sig, dot, memory, gain_mem)
    begun = project_first(mixed_keep, out_weight)
    mixed_recv = permute(mixed_send, "c", (1, 0))
    return project_last(mixed_recv, begun, out_weight)


def solution(mesh):
    finer = Mesh(mesh.devices.reshape(4, 8, 4, 2), AXES)
    in_specs = (P(AXES, None), P(AXES, None), P(AXES, None), P(), P(), P())
    return jax.shard_map(
        layer, mesh=finer, in_specs=in_specs, out_specs=P(AXES, None), check_vma=False
    )
```

```python
import functools

import jax
import jax.numpy as jnp
from jax import lax
from jax.experimental import pallas as pl
from jax.experimental.pallas import tpu as pltpu
from jax.sharding import Mesh
from jax.sharding import PartitionSpec as P


HEAD = 128
GROUP = 4
HEADS = 8
AXES = ("sx", "sz", "y", "c")
EXP_SCALE = float(HEAD) ** (-0.5) * 1.4426950408889634
NT = (((1,), (1,)), ((), ()))
TN = (((0,), (0,)), ((), ()))
BF16 = jnp.bfloat16
F32 = jnp.float32
VM = pl.BlockSpec(memory_space=pltpu.VMEM)
HBM = pl.BlockSpec(memory_space=pltpu.HBM)


def placed(x, space=pltpu.VMEM):
    return pltpu.with_memory_space_constraint(x, space)


def kernel_call(body, outs, args, limit, flops=0, nbytes=0, trans=0, specs=None, **more):
    specs = specs or [VM] * len(args)
    args = [placed(a, s.memory_space) for a, s in zip(args, specs)]
    return pl.pallas_call(
        body,
        out_shape=[pltpu.VMEM(shape, dtype) for shape, dtype in outs],
        in_specs=specs,
        out_specs=[VM] * len(outs),
        compiler_params=pltpu.CompilerParams(vmem_limit_bytes=limit * 2**20),
        cost_estimate=pl.CostEstimate(flops=flops, bytes_accessed=nbytes, transcendentals=trans),
        **more,
    )(*args)


def feature_map(x):
    return jnp.where(x > 0, x + 1.0, jnp.exp(jnp.minimum(x, 0.0)))


def prep_kernel(k, v, q, kv_own, q_own, sems):
    half = k.shape[1] // 2
    c = lax.axis_index("c")
    moves = [(k, kv_own.at[:, :half], half), (v, kv_own.at[:, half:], half), (q, q_own, 4 * half)]
    copies = []
    for n, (src, dst, width) in enumerate(moves):
        cols = pl.ds(pl.multiple_of(c * width, width), width)
        copies.append(pltpu.make_async_copy(src.at[:, cols], dst, sems.at[n]))
        copies[-1].start()
    for copy in copies:
        copy.wait()


def prep(k, v, q):
    outs = [(k.shape, BF16), ((q.shape[0], q.shape[1] // 2), BF16)]
    return kernel_call(
        prep_kernel, outs, (k, v, q), 8, nbytes=2**21, specs=[HBM] * 3,
        scratch_shapes=[pltpu.SemaphoreType.DMA((3,))],
    )


def part_kernel(kv_own, k_recv, v_recv, both, total, sent):
    rows, half = k_recv.shape[0], k_recv.shape[1] // 2
    c = lax.axis_index("c")
    own = pl.ds(pl.multiple_of(c * half, half), half)
    both[pl.ds(pl.multiple_of(c * rows, rows), rows), :] = kv_own[...]
    for i, ref in enumerate((k_recv, v_recv)):
        at = pl.ds(pl.multiple_of(rows - c * rows, rows), rows)
        both[at, i * half : (i + 1) * half] = ref[:, own]
    for g in range(2):
        kk = slice(g * HEAD, (g + 1) * HEAD)
        vv = slice(half + g * HEAD, half + (g + 1) * HEAD)
        sig = feature_map(both[:, kk].astype(F32)).astype(BF16)
        acc = lax.dot_general(sig, both[:, vv], TN, preferred_element_type=F32)
        total[kk, :] = acc
        sent[kk, :] = acc.astype(BF16)


def part(kv_own, k_recv, v_recv):
    rows, cols = kv_own.shape
    outs = [((2 * rows, cols), BF16), ((cols // 2, HEAD), F32), ((cols // 2, HEAD), BF16)]
    return kernel_call(part_kernel, outs, (kv_own, k_recv, v_recv), 8, 2**26, 2**21)


def tiles(rows=256, size=128):
    for g in range(2):
        for b in range(2):
            for j in range(GROUP):
                h = g * GROUP + j
                cols, wide = slice(h * HEAD, (h + 1) * HEAD), slice(2 * h * HEAD, 2 * (h + 1) * HEAD)
                for r in range(0, rows, size):
                    yield g, b, h, slice(r, r + size), cols, wide


def head_of(q, h):
    if q.shape[1] == HEADS * HEAD:
        return slice(h * HEAD, (h + 1) * HEAD)
    first = lax.axis_index("c") * (HEADS * HEAD) + h * HEAD
    return pl.ds(pl.multiple_of(first, HEAD), HEAD)


def fill_ones(kv, v_ones):
    for g in range(2):
        v = kv[:, (2 + g) * HEAD : (3 + g) * HEAD]
        v_ones[g] = jnp.concatenate([v, jnp.ones_like(v)], axis=1)


def scores(q_refs, kv, g, b, h, r):
    q, k = q_refs[b][r, head_of(q_refs[b], h)], kv[:, g * HEAD : (g + 1) * HEAD]
    return lax.dot_general(q, k, NT, preferred_element_type=F32)


def weigh(s, new, v_ones):
    w = [
        jnp.exp2((s[:, n : n + HEAD] - new) * EXP_SCALE).astype(BF16)
        for n in range(0, s.shape[1], HEAD)
    ]
    return jnp.dot(jnp.concatenate(w, axis=1), v_ones, preferred_element_type=F32)


def first_kernel(q_keep, q_recv, kv, ext, top, v_ones):
    rows = q_keep.shape[0]
    fill_ones(kv, v_ones)
    c = lax.axis_index("c")
    for g, b, h, r, cols, wide in tiles():
        s = scores((q_keep, q_recv), kv, g, b, h, r)
        first = (c if b == 0 else 1 - c) * rows + r.start
        row = lax.broadcasted_iota(jnp.int32, s.shape, 0) + first
        s = jnp.where(row >= lax.broadcasted_iota(jnp.int32, s.shape, 1), s, -1e30)
        m = jnp.broadcast_to(jnp.max(s, axis=-1, keepdims=True), (s.shape[0], HEAD))
        ext[b, r, wide] = weigh(s, m, v_ones[g])
        top[b, r, cols] = m


def state(rows):
    return [((2, rows, 2 * HEADS * HEAD), F32), ((2, rows, HEADS * HEAD), F32)]


def attend_first(q_keep, q_recv, kv):
    rows, keys = q_keep.shape[0], kv.shape[0]
    count = 2 * HEADS * rows * keys
    return kernel_call(
        first_kernel, state(rows), (q_keep, q_recv, kv), 20,
        4 * count * HEAD, 2**22, count,
        scratch_shapes=[pltpu.VMEM((2, keys, 2 * HEAD), BF16)],
    )


def fold_chunk(q_refs, kv, v_ones, ext, top):
    fill_ones(kv, v_ones)
    for g, b, h, r, cols, wide in tiles():
        s = scores(q_refs, kv, g, b, h, r)
        old = top[b, r, cols]
        new = jnp.maximum(old, jnp.max(s, axis=-1, keepdims=True))
        alpha = jnp.exp2((old - new) * EXP_SCALE)
        total = ext[b, r, wide] * jnp.concatenate([alpha, alpha], axis=1) + weigh(s, new, v_ones[g])
        yield b, h, r, cols, wide, new, total


def next_kernel(first_y, q_keep, q_recv, kv, ext_in, top_in, ext, top, v_ones):
    @pl.when(lax.axis_index("y") >= first_y)
    def _():
        for b, h, r, cols, wide, new, total in fold_chunk((q_keep, q_recv), kv, v_ones, ext, top):
            ext[b, r, wide] = total
            top[b, r, cols] = new


def attend_next(first_y, q_keep, q_recv, kv, ext, top):
    rows, keys = q_keep.shape[0], kv.shape[0]
    count = 2 * HEADS * rows * keys
    return kernel_call(
        functools.partial(next_kernel, first_y), state(rows), (q_keep, q_recv, kv, ext, top),
        20, 4 * count * HEAD, 2**22, count,
        scratch_shapes=[pltpu.VMEM((2, keys, 2 * HEAD), BF16)],
        input_output_aliases={3: 0, 4: 1},
    )


def head_norm(x, gain):
    return x * (0.5 * lax.rsqrt(jnp.mean(x * x, axis=-1, keepdims=True) + 1e-06)) * gain


def last_kernel(q_keep, q_recv, kv, ext, top, gain, out, v_ones):
    y, c = lax.axis_index("y"), lax.axis_index("c")
    own = pl.multiple_of(c * HEADS, HEADS)

    def put(b, h, r, cols, total):
        acc, den = total[:, :HEAD], total[:, HEAD:]
        square = jnp.mean(acc * acc + 1e-06 * (den * den), axis=-1, keepdims=True)
        out[b, r, cols] = acc * (0.5 * lax.rsqrt(square)) * gain[pl.ds(own + h, 1), :]

    @pl.when(y >= 2)
    def _():
        for b, h, r, cols, wide, new, total in fold_chunk((q_keep, q_recv), kv, v_ones, ext, top):
            put(b, h, r, cols, total)

    @pl.when(y < 2)
    def _():
        for g, b, h, r, cols, wide in tiles():
            put(b, h, r, cols, ext[b, r, wide])


def attend_last(q_keep, q_recv, far, ext, top, gain):
    rows, keys = q_keep.shape[0], far.shape[0]
    count = 2 * HEADS * rows * keys
    outs = [((2, rows, HEADS * HEAD), F32)]
    return kernel_call(
        last_kernel, outs, (q_keep, q_recv, far, ext, top, gain), 20,
        4 * count * HEAD, 2**22, count,
        scratch_shapes=[pltpu.VMEM((2, keys, 2 * HEAD), BF16)],
    )[0]


def sig_kernel(q_keep, q_recv, sig):
    for b, q in enumerate((q_keep, q_recv)):
        for h in range(HEADS):
            x = q[:, head_of(q, h)].astype(F32)
            sig[b, :, h * HEAD : (h + 1) * HEAD] = feature_map(x).astype(BF16)


def mix_rows(b, sig, dot, parts, gain, out):
    own = pl.multiple_of(lax.axis_index("c") * HEADS, HEADS)
    terms = [ref[...].astype(F32) for ref in parts]
    memory = ((terms[0] + terms[1]) + (terms[2] + terms[3])).astype(BF16)
    for h in range(HEADS):
        cols, g = slice(h * HEAD, (h + 1) * HEAD), h // GROUP
        read = jnp.dot(
            sig[b, :, cols], memory[g * HEAD : (g + 1) * HEAD], preferred_element_type=F32
        )
        mixed = head_norm(read, gain[pl.ds(own + h, 1), :]) + dot[b, :, cols]
        out[:, cols] = mixed.astype(BF16)


def mix_send_kernel(sig, dot, m0, m1, m2, m3, gain, out):
    mix_rows(1, sig, dot, (m0, m1, m2, m3), gain, out)


def mix_send(sig, dot, memory, gain):
    outs = [(sig.shape[1:], BF16)]
    args = (sig, dot, *memory, gain)
    return kernel_call(mix_send_kernel, outs, args, 12, 2**26, 2**21)[0]


def project_own_kernel(core, sig, dot, m0, m1, m2, m3, gain, weight, *more):
    out, keep = more[-2:]

    @pl.when(lax.axis_index("c") == core)
    def _():
        mix_rows(0, sig, dot, (m0, m1, m2, m3), gain, keep)
        half = keep.shape[1]
        own = pl.multiple_of(core * half, half)
        for n in range(0, weight.shape[1], 512):
            out[:, n : n + 512] = jnp.dot(
                keep[...], weight[pl.ds(own, half), n : n + 512], preferred_element_type=F32
            )


def project_own(core, sig, dot, memory, gain, weight, begun):
    rows, width = sig.shape[1], weight.shape[1]
    args = (sig, dot, *memory, gain, weight, *begun)
    return kernel_call(
        functools.partial(project_own_kernel, core), [((rows, width), F32)], args, 16,
        2**30, 2**23, scratch_shapes=[pltpu.VMEM(sig.shape[1:], BF16)],
        input_output_aliases={8: 0} if begun else {},
    )


def project_last_kernel(x, begun, weight, out, stage, sems):
    half, width = x.shape[1], 256
    other = pl.multiple_of(half - lax.axis_index("c") * half, half)
    copies = []
    for i in range(out.shape[1] // width):
        n = slice(i * width, (i + 1) * width)
        total = jnp.dot(x[...], weight[pl.ds(other, half), n], preferred_element_type=F32)
        stage[:, n] = (begun[:, n] + total).astype(BF16)
        copies.append(pltpu.make_async_copy(stage.at[:, n], out.at[:, n], sems.at[i]))
        copies[-1].start()
    for copy in copies:
        copy.wait()


def project_last(x, begun, weight):
    shape = begun.shape
    return pl.pallas_call(
        project_last_kernel,
        out_shape=pltpu.HBM(shape, BF16),
        in_specs=[VM] * 3,
        out_specs=HBM,
        scratch_shapes=[pltpu.VMEM(shape, BF16), pltpu.SemaphoreType.DMA((shape[1] // 256,))],
        name="project_last",
        compiler_params=pltpu.CompilerParams(vmem_limit_bytes=16 * 2**20),
        cost_estimate=pl.CostEstimate(flops=2**30, bytes_accessed=2**23, transcendentals=0),
    )(*[placed(a) for a in (x, begun, weight)])


def permute(x, axis, partner):
    return lax.ppermute(x, axis, list(enumerate(partner)))


def shift(x, axis, step, size):
    return permute(x, axis, [(i + step) % size for i in range(size)])


def add_kernel(axis, level, total, before, got, before_out, *more):
    upper = ((lax.axis_index(axis) >> level) & 1).astype(F32)
    term = got[...].astype(F32)
    earlier = before[...] + term * upper
    before_out[...] = earlier.astype(before_out.dtype)
    if more:
        total_out, sent = more
        summed = total[...] + term
        total_out[...] = summed
        sent[...] = summed.astype(BF16)


def earlier_memory(total, sent):
    before = jnp.zeros_like(total)
    shape = total.shape
    steps = (
        ("sz", 0, [i ^ 1 for i in range(8)], "z1"),
        ("sz", 1, [i ^ 2 for i in range(8)], "z2"),
        ("sz", 2, [7 - i for i in range(8)], "z3"),
        ("sx", 0, [i ^ 1 for i in range(4)], "x1"),
        ("sx", 1, [3 - i for i in range(4)], "x2"),
    )
    for axis, level, partner, name in steps:
        last = name == "x2"
        got = permute(sent, axis, partner)
        outs = [(shape, BF16)] if last else [(shape, F32), (shape, F32), (shape, BF16)]
        result = kernel_call(
            functools.partial(add_kernel, axis, level), outs, (total, before, got),
            4, 2**17, 2**18,
        )
        if last:
            return result[0]
        before, total, sent = result


def layer(queries, keys, values, gain_mem, gain_dot, out_weight):
    k_recv = permute(keys, "c", (1, 0))
    v_recv = permute(values, "c", (1, 0))
    q_recv = permute(queries, "c", (1, 0))
    kv_own, q_own = prep(keys, values, queries)
    kv, total, sent = part(kv_own, k_recv, v_recv)
    left = shift(kv, "y", 1, 4)
    right = shift(kv, "y", 3, 4)
    far = permute(kv, "y", [i ^ 2 for i in range(4)])
    mine = earlier_memory(total, sent)
    memory = [mine] + [permute(mine, "y", [i ^ n for i in range(4)]) for n in (1, 2, 3)]
    ext, top = attend_first(q_own, q_recv, kv)
    ext, top = attend_next(1, q_own, q_recv, left, ext, top)
    ext, top = attend_next(3, q_own, q_recv, right, ext, top)
    gain_dot = gain_dot.reshape(2 * HEADS, HEAD)
    gain_mem = gain_mem.reshape(2 * HEADS, HEAD)
    dot = attend_last(q_own, q_recv, far, ext, top, gain_dot)
    shape = (2, *q_own.shape)
    sig = kernel_call(sig_kernel, [(shape, BF16)], (q_own, q_recv), 8, 2**21, 2**22)[0]
    mixed_send = mix_send(sig, dot, memory, gain_mem)
    begun = project_own(1, sig, dot, memory, gain_mem, out_weight, [])
    begun = project_own(0, sig, dot, memory, gain_mem, out_weight, begun)[0]
    mixed_recv = permute(mixed_send, "c", (1, 0))
    return project_last(mixed_recv, begun, out_weight)


def solution(mesh):
    finer = Mesh(mesh.devices.reshape(4, 8, 4, 2), AXES)
    in_specs = (P(AXES, None), P(AXES, None), P(AXES, None), P(), P(), P())
    return jax.shard_map(
        layer, mesh=finer, in_specs=in_specs, out_specs=P(AXES, None), check_vma=False
    )
```

```python
import functools

import jax
import jax.numpy as jnp
from jax import lax
from jax.experimental import pallas as pl
from jax.experimental.pallas import tpu as pltpu
from jax.sharding import Mesh
from jax.sharding import PartitionSpec as P


HEAD = 128
GROUP = 4
HEADS = 8
AXES = ("sx", "sz", "y", "c")
EXP_SCALE = float(HEAD) ** (-0.5) * 1.4426950408889634
NT = (((1,), (1,)), ((), ()))
TN = (((0,), (0,)), ((), ()))
BF16 = jnp.bfloat16
F32 = jnp.float32
VM = pl.BlockSpec(memory_space=pltpu.VMEM)
HBM = pl.BlockSpec(memory_space=pltpu.HBM)


def placed(x, space=pltpu.VMEM):
    return pltpu.with_memory_space_constraint(x, space)


def kernel_call(body, outs, args, limit, flops=0, nbytes=0, trans=0, specs=None, **more):
    specs = specs or [VM] * len(args)
    args = [placed(a, s.memory_space) for a, s in zip(args, specs)]
    return pl.pallas_call(
        body,
        out_shape=[pltpu.VMEM(shape, dtype) for shape, dtype in outs],
        in_specs=specs,
        out_specs=[VM] * len(outs),
        compiler_params=pltpu.CompilerParams(vmem_limit_bytes=limit * 2**20),
        cost_estimate=pl.CostEstimate(flops=flops, bytes_accessed=nbytes, transcendentals=trans),
        **more,
    )(*args)


def feature_map(x):
    return jnp.where(x > 0, x + 1.0, jnp.exp(jnp.minimum(x, 0.0)))


def prep_kernel(k, v, q, kv_own, q_own, sems):
    half = k.shape[1] // 2
    c = lax.axis_index("c")
    moves = [(k, kv_own.at[:, :half], half), (v, kv_own.at[:, half:], half), (q, q_own, 4 * half)]
    copies = []
    for n, (src, dst, width) in enumerate(moves):
        cols = pl.ds(pl.multiple_of(c * width, width), width)
        copies.append(pltpu.make_async_copy(src.at[:, cols], dst, sems.at[n]))
        copies[-1].start()
    for copy in copies:
        copy.wait()


def prep(k, v, q):
    outs = [(k.shape, BF16), ((q.shape[0], q.shape[1] // 2), BF16)]
    return kernel_call(
        prep_kernel, outs, (k, v, q), 8, nbytes=2**21, specs=[HBM] * 3,
        scratch_shapes=[pltpu.SemaphoreType.DMA((3,))],
    )


def part_kernel(kv_own, k_recv, v_recv, both, total, sent):
    rows, half = k_recv.shape[0], k_recv.shape[1] // 2
    c = lax.axis_index("c")
    own = pl.ds(pl.multiple_of(c * half, half), half)
    both[pl.ds(pl.multiple_of(c * rows, rows), rows), :] = kv_own[...]
    for i, ref in enumerate((k_recv, v_recv)):
        at = pl.ds(pl.multiple_of(rows - c * rows, rows), rows)
        both[at, i * half : (i + 1) * half] = ref[:, own]
    for g in range(2):
        kk = slice(g * HEAD, (g + 1) * HEAD)
        vv = slice(half + g * HEAD, half + (g + 1) * HEAD)
        sig = feature_map(both[:, kk].astype(F32)).astype(BF16)
        acc = lax.dot_general(sig, both[:, vv], TN, preferred_element_type=F32)
        total[kk, :] = acc
        sent[kk, :] = acc.astype(BF16)


def part(kv_own, k_recv, v_recv):
    rows, cols = kv_own.shape
    outs = [((2 * rows, cols), BF16), ((cols // 2, HEAD), F32), ((cols // 2, HEAD), BF16)]
    return kernel_call(part_kernel, outs, (kv_own, k_recv, v_recv), 8, 2**26, 2**21)


def tiles(rows=256, size=128):
    for g in range(2):
        for b in range(2):
            for j in range(GROUP):
                h = g * GROUP + j
                cols, wide = slice(h * HEAD, (h + 1) * HEAD), slice(2 * h * HEAD, 2 * (h + 1) * HEAD)
                for r in range(0, rows, size):
                    yield g, b, h, slice(r, r + size), cols, wide


def head_of(q, h):
    if q.shape[1] == HEADS * HEAD:
        return slice(h * HEAD, (h + 1) * HEAD)
    first = lax.axis_index("c") * (HEADS * HEAD) + h * HEAD
    return pl.ds(pl.multiple_of(first, HEAD), HEAD)


def fill_ones(kv, v_ones):
    for g in range(2):
        v = kv[:, (2 + g) * HEAD : (3 + g) * HEAD]
        v_ones[g] = jnp.concatenate([v, jnp.ones_like(v)], axis=1)


def scores(q_refs, kv, g, b, h, r):
    q, k = q_refs[b][r, head_of(q_refs[b], h)], kv[:, g * HEAD : (g + 1) * HEAD]
    return lax.dot_general(q, k, NT, preferred_element_type=F32)


def weigh(s, new, v_ones):
    w = [
        jnp.exp2((s[:, n : n + HEAD] - new) * EXP_SCALE).astype(BF16)
        for n in range(0, s.shape[1], HEAD)
    ]
    return jnp.dot(jnp.concatenate(w, axis=1), v_ones, preferred_element_type=F32)


def first_kernel(q_keep, q_recv, kv, ext, top, v_ones):
    rows = q_keep.shape[0]
    fill_ones(kv, v_ones)
    c = lax.axis_index("c")
    for g, b, h, r, cols, wide in tiles():
        s = scores((q_keep, q_recv), kv, g, b, h, r)
        first = (c if b == 0 else 1 - c) * rows + r.start
        row = lax.broadcasted_iota(jnp.int32, s.shape, 0) + first
        s = jnp.where(row >= lax.broadcasted_iota(jnp.int32, s.shape, 1), s, -1e30)
        m = jnp.broadcast_to(jnp.max(s, axis=-1, keepdims=True), (s.shape[0], HEAD))
        ext[b, r, wide] = weigh(s, m, v_ones[g])
        top[b, r, cols] = m


def state(rows):
    return [((2, rows, 2 * HEADS * HEAD), F32), ((2, rows, HEADS * HEAD), F32)]


def attend_first(q_keep, q_recv, kv):
    rows, keys = q_keep.shape[0], kv.shape[0]
    count = 2 * HEADS * rows * keys
    return kernel_call(
        first_kernel, state(rows), (q_keep, q_recv, kv), 20,
        4 * count * HEAD, 2**22, count,
        scratch_shapes=[pltpu.VMEM((2, keys, 2 * HEAD), BF16)],
    )


def fold_chunk(q_refs, kv, v_ones, ext, top):
    fill_ones(kv, v_ones)
    for g, b, h, r, cols, wide in tiles():
        s = scores(q_refs, kv, g, b, h, r)
        old = top[b, r, cols]
        new = jnp.maximum(old, jnp.max(s, axis=-1, keepdims=True))
        alpha = jnp.exp2((old - new) * EXP_SCALE)
        total = ext[b, r, wide] * jnp.concatenate([alpha, alpha], axis=1) + weigh(s, new, v_ones[g])
        yield b, h, r, cols, wide, new, total


def next_kernel(first_y, q_keep, q_recv, kv, ext_in, top_in, ext, top, v_ones):
    @pl.when(lax.axis_index("y") >= first_y)
    def _():
        for b, h, r, cols, wide, new, total in fold_chunk((q_keep, q_recv), kv, v_ones, ext, top):
            ext[b, r, wide] = total
            top[b, r, cols] = new


def attend_next(first_y, q_keep, q_recv, kv, ext, top):
    rows, keys = q_keep.shape[0], kv.shape[0]
    count = 2 * HEADS * rows * keys
    return kernel_call(
        functools.partial(next_kernel, first_y), state(rows), (q_keep, q_recv, kv, ext, top),
        20, 4 * count * HEAD, 2**22, count,
        scratch_shapes=[pltpu.VMEM((2, keys, 2 * HEAD), BF16)],
        input_output_aliases={3: 0, 4: 1},
    )


def head_norm(x, gain):
    return x * (0.5 * lax.rsqrt(jnp.mean(x * x, axis=-1, keepdims=True) + 1e-06)) * gain


def last_kernel(q_keep, q_recv, kv, ext, top, gain, out, v_ones):
    y, c = lax.axis_index("y"), lax.axis_index("c")
    own = pl.multiple_of(c * HEADS, HEADS)

    def put(b, h, r, cols, total):
        acc, den = total[:, :HEAD], total[:, HEAD:]
        square = jnp.mean(acc * acc + 1e-06 * (den * den), axis=-1, keepdims=True)
        out[b, r, cols] = acc * (0.5 * lax.rsqrt(square)) * gain[pl.ds(own + h, 1), :]

    @pl.when(y >= 2)
    def _():
        for b, h, r, cols, wide, new, total in fold_chunk((q_keep, q_recv), kv, v_ones, ext, top):
            put(b, h, r, cols, total)

    @pl.when(y < 2)
    def _():
        for g, b, h, r, cols, wide in tiles():
            put(b, h, r, cols, ext[b, r, wide])


def attend_last(q_keep, q_recv, far, ext, top, gain):
    rows, keys = q_keep.shape[0], far.shape[0]
    count = 2 * HEADS * rows * keys
    outs = [((2, rows, HEADS * HEAD), F32)]
    return kernel_call(
        last_kernel, outs, (q_keep, q_recv, far, ext, top, gain), 20,
        4 * count * HEAD, 2**22, count,
        scratch_shapes=[pltpu.VMEM((2, keys, 2 * HEAD), BF16)],
    )[0]


def sig_kernel(q_keep, q_recv, sig):
    for b, q in enumerate((q_keep, q_recv)):
        for h in range(HEADS):
            x = q[:, head_of(q, h)].astype(F32)
            sig[b, :, h * HEAD : (h + 1) * HEAD] = feature_map(x).astype(BF16)


def mix_rows(b, r, sig, dot, parts, gain, out):
    own = pl.multiple_of(lax.axis_index("c") * HEADS, HEADS)
    terms = [ref[...].astype(F32) for ref in parts]
    memory = ((terms[0] + terms[1]) + (terms[2] + terms[3])).astype(BF16)
    for h in range(HEADS):
        cols, g = slice(h * HEAD, (h + 1) * HEAD), h // GROUP
        read = jnp.dot(
            sig[b, r, cols], memory[g * HEAD : (g + 1) * HEAD], preferred_element_type=F32
        )
        mixed = head_norm(read, gain[pl.ds(own + h, 1), :]) + dot[b, r, cols]
        out[:, cols] = mixed.astype(BF16)


def mix_send_kernel(r, core, sig, dot, m0, m1, m2, m3, gain, *more):
    here = True if core is None else lax.axis_index("c") == core

    @pl.when(here)
    def _():
        mix_rows(1, r, sig, dot, (m0, m1, m2, m3), gain, more[-1])


def mix_send(part, core, sig, dot, memory, gain, begun):
    half = sig.shape[1] // 2
    outs = [((half, sig.shape[2]), BF16)]
    body = functools.partial(mix_send_kernel, slice(part * half, (part + 1) * half), core)
    return kernel_call(
        body, outs, (sig, dot, *memory, gain, *begun), 12, 2**25, 2**20,
        input_output_aliases={7: 0} if begun else {},
    )


def project_own_kernel(core, sig, dot, m0, m1, m2, m3, gain, weight, *more):
    out, keep = more[-2:]

    @pl.when(lax.axis_index("c") == core)
    def _():
        mix_rows(0, slice(None), sig, dot, (m0, m1, m2, m3), gain, keep)
        half = keep.shape[1]
        own = pl.multiple_of(core * half, half)
        for n in range(0, weight.shape[1], 512):
            out[:, n : n + 512] = jnp.dot(
                keep[...], weight[pl.ds(own, half), n : n + 512], preferred_element_type=F32
            )


def project_own(core, sig, dot, memory, gain, weight, begun):
    rows, width = sig.shape[1], weight.shape[1]
    args = (sig, dot, *memory, gain, weight, *begun)
    return kernel_call(
        functools.partial(project_own_kernel, core), [((rows, width), F32)], args, 16,
        2**30, 2**23, scratch_shapes=[pltpu.VMEM(sig.shape[1:], BF16)],
        input_output_aliases={8: 0} if begun else {},
    )


def project_rows(part, x, begun, weight):
    rows, half = x.shape
    other = pl.multiple_of(half - lax.axis_index("c") * half, half)
    for first in range(0, weight.shape[1], 256):
        n = slice(first, first + 256)
        total = jnp.dot(x[...], weight[pl.ds(other, half), n], preferred_element_type=F32)
        yield n, (begun[part * rows : (part + 1) * rows, n] + total).astype(BF16)


def project_a_kernel(x, begun, weight, out):
    for n, total in project_rows(0, x, begun, weight):
        out[:, n] = total


def project_b_kernel(x, begun, weight, done, out, stage, sems):
    rows = x.shape[0]
    copies = [pltpu.make_async_copy(done, out.at[:rows, :], sems.at[0])]
    copies[0].start()
    for i, (n, total) in enumerate(project_rows(1, x, begun, weight)):
        stage[:, n] = total
        if i % 2:
            pair = slice(n.stop - 512, n.stop)
            dst = out.at[rows:, pair]
            copies.append(pltpu.make_async_copy(stage.at[:, pair], dst, sems.at[1 + i // 2]))
            copies[-1].start()
    for copy in copies:
        copy.wait()


def project_last(x_a, x_b, begun, weight):
    shape, rows = begun.shape, x_a.shape[0]
    outs = [((rows, shape[1]), BF16)]
    done = kernel_call(project_a_kernel, outs, (x_a, begun, weight), 16, 2**29, 2**22)
    return pl.pallas_call(
        project_b_kernel,
        out_shape=pltpu.HBM(shape, BF16),
        in_specs=[VM] * 4,
        out_specs=HBM,
        scratch_shapes=[
            pltpu.VMEM((rows, shape[1]), BF16),
            pltpu.SemaphoreType.DMA((1 + shape[1] // 512,)),
        ],
        name="project_b",
        compiler_params=pltpu.CompilerParams(vmem_limit_bytes=16 * 2**20),
        cost_estimate=pl.CostEstimate(flops=2**29, bytes_accessed=2**22, transcendentals=0),
    )(*[placed(a) for a in (x_b, begun, weight, done[0])])


def permute(x, axis, partner):
    return lax.ppermute(x, axis, list(enumerate(partner)))


def shift(x, axis, step, size):
    return permute(x, axis, [(i + step) % size for i in range(size)])


def add_kernel(axis, level, total, before, got, before_out, *more):
    upper = ((lax.axis_index(axis) >> level) & 1).astype(F32)
    term = got[...].astype(F32)
    earlier = before[...] + term * upper
    before_out[...] = earlier.astype(before_out.dtype)
    if more:
        total_out, sent = more
        summed = total[...] + term
        total_out[...] = summed
        sent[...] = summed.astype(BF16)


def earlier_memory(total, sent):
    before = jnp.zeros_like(total)
    shape = total.shape
    steps = (
        ("sz", 0, [i ^ 1 for i in range(8)], "z1"),
        ("sz", 1, [i ^ 2 for i in range(8)], "z2"),
        ("sz", 2, [7 - i for i in range(8)], "z3"),
        ("sx", 0, [i ^ 1 for i in range(4)], "x1"),
        ("sx", 1, [3 - i for i in range(4)], "x2"),
    )
    for axis, level, partner, name in steps:
        last = name == "x2"
        got = permute(sent, axis, partner)
        outs = [(shape, BF16)] if last else [(shape, F32), (shape, F32), (shape, BF16)]
        result = kernel_call(
            functools.partial(add_kernel, axis, level), outs, (total, before, got),
            4, 2**17, 2**18,
        )
        if last:
            return result[0]
        before, total, sent = result


def layer(queries, keys, values, gain_mem, gain_dot, out_weight):
    k_recv = permute(keys, "c", (1, 0))
    v_recv = permute(values, "c", (1, 0))
    q_recv = permute(queries, "c", (1, 0))
    kv_own, q_own = prep(keys, values, queries)
    kv, total, sent = part(kv_own, k_recv, v_recv)
    left = shift(kv, "y", 1, 4)
    right = shift(kv, "y", 3, 4)
    far = permute(kv, "y", [i ^ 2 for i in range(4)])
    mine = earlier_memory(total, sent)
    memory = [mine] + [permute(mine, "y", [i ^ n for i in range(4)]) for n in (1, 2, 3)]
    ext, top = attend_first(q_own, q_recv, kv)
    ext, top = attend_next(1, q_own, q_recv, left, ext, top)
    ext, top = attend_next(3, q_own, q_recv, right, ext, top)
    gain_dot = gain_dot.reshape(2 * HEADS, HEAD)
    gain_mem = gain_mem.reshape(2 * HEADS, HEAD)
    dot = attend_last(q_own, q_recv, far, ext, top, gain_dot)
    shape = (2, *q_own.shape)
    sig = kernel_call(sig_kernel, [(shape, BF16)], (q_own, q_recv), 8, 2**21, 2**22)[0]
    mixed_a = mix_send(0, None, sig, dot, memory, gain_mem, [])[0]
    mixed_b = mix_send(1, 1, sig, dot, memory, gain_mem, [])
    mixed_b = mix_send(1, 0, sig, dot, memory, gain_mem, mixed_b)[0]
    begun = project_own(1, sig, dot, memory, gain_mem, out_weight, [])
    begun = project_own(0, sig, dot, memory, gain_mem, out_weight, begun)[0]
    mixed_a = permute(mixed_a, "c", (1, 0))
    mixed_b = permute(mixed_b, "c", (1, 0))
    return project_last(mixed_a, mixed_b, begun, out_weight)


def solution(mesh):
    finer = Mesh(mesh.devices.reshape(4, 8, 4, 2), AXES)
    in_specs = (P(AXES, None), P(AXES, None), P(AXES, None), P(), P(), P())
    return jax.shard_map(
        layer, mesh=finer, in_specs=in_specs, out_specs=P(AXES, None), check_vma=False
    )
```
